32 devices in a mesh: dev: 32 (over z, y, x, core).
Axes of the slice: x: 2, y: 2, z: 4, core: 2. Of those that a mesh axis runs over, the one named last changes fastest.
Arguments:
- tokens: bfloat16 [64, 512, 768], P(None, 'dev'), may hold values from -6 to 6
- cotangent: bfloat16 [18432, 768], P('dev'), may hold values from -6 to 6
- lengths: int32 [64], replicated, may hold values from 1 to 512, as said below
- dealing: int32 [64], replicated, may hold values from 0 to 63, as said below
- w_query: bfloat16 [768, 768], P('dev'), may hold values from -0.21875 to 0.21875
- w_key: bfloat16 [768, 768], P('dev'), may hold values from -0.21875 to 0.21875
- w_value: bfloat16 [768, 768], P('dev'), may hold values from -0.21875 to 0.21875
- w_out: bfloat16 [768, 768], P('dev'), may hold values from -1.75 to 1.75
- b_query: bfloat16 [768], P('dev'), may hold values from -3 to 3
- b_value: bfloat16 [768], P('dev'), may hold values from -3 to 3
- b_out: bfloat16 [768], P('dev'), may hold values from -3 to 3
- norm1_gain: bfloat16 [768], P('dev'), may hold values from 0.5 to 1.5
- norm1_bias: bfloat16 [768], P('dev'), may hold values from -3 to 3
- w_up: bfloat16 [768, 3072], P('dev'), may hold values from -0.21875 to 0.21875
- b_up: bfloat16 [3072], P('dev'), may hold values from -3 to 3
- w_down: bfloat16 [3072, 768], P('dev'), may hold values from -0.109375 to 0.109375
- b_down: bfloat16 [768], P('dev'), may hold values from -3 to 3
- norm2_gain: bfloat16 [768], P('dev'), may hold values from 0.5 to 1.5
- norm2_bias: bfloat16 [768], P('dev'), may hold values from -3 to 3
Outputs:
- layer_out: bfloat16 [18432, 768], P('dev')
- input_grad: bfloat16 [64, 512, 768], P(None, 'dev')
- grad_w_query: float32 [768, 768], P('dev')
- grad_w_key: float32 [768, 768], P('dev')
- grad_w_value: float32 [768, 768], P('dev')
- grad_w_out: float32 [768, 768], P('dev')
- grad_b_query: float32 [768], P('dev')
- grad_b_value: float32 [768], P('dev')
- grad_b_out: float32 [768], P('dev')
- grad_norm1_gain: float32 [768], P('dev')
- grad_norm1_bias: float32 [768], P('dev')
- grad_w_up: float32 [768, 3072], P('dev')
- grad_b_up: float32 [3072], P('dev')
- grad_w_down: float32 [3072, 768], P('dev')
- grad_b_down: float32 [768], P('dev')
- grad_norm2_gain: float32 [768], P('dev')
- grad_norm2_bias: float32 [768], P('dev')
The draws below stay inside these ranges and needn't reach their ends.
Inputs may be any that keep to these rules, and one draw needn't show every extreme that they name: lengths[s] is sequence s's token count. Slots 2 * k and 2 * k + 1 of the dealt order hold at most 576 tokens together, so the 2 sequences of one device hold at most 576; some device holds exactly 576, and some sequence has exactly 512 tokens. A permutation: dealing[q] is the sequence in slot q; slots 2 * i to 2 * i + 1 go to device i and are packed there in slot order.
All inputs are finite; a program needn't handle non-finite values.
Results may differ from the reference program's by a relative error of at most 0.014.
Values may be sent and summed in bfloat16 or wider, within the bound.
No kernel may reach another device: no remote copies, remote signals or barrier semaphores. Data moves between devices by JAX's collectives and lax.ppermute only.
A program may use at most 128 MiB of HBM per device.

```python
import jax
import jax.numpy as jnp
from jax import lax

D = 768
HEADS = 12
HEAD_DIM = 64
FF = 3072
MAXLEN = 512
SPD = 2
PAIRSUM = 576
CAP = 576
NSEQ = 64
PACKED = 18432
N_DEV = 32


def dealt_plan(key):
    base = jax.random.fold_in(key, 17)
    key_first, key_slack, key_pick, key_coin, key_order = jax.random.split(base, 5)
    pair_count = NSEQ // 2
    pairs_each = SPD // 2
    extra_room = PAIRSUM - MAXLEN
    pair_ids = jnp.arange(pair_count, dtype=jnp.int32)
    first_len = jax.random.randint(key_first, (pair_count,), extra_room, MAXLEN + 1, dtype=jnp.int32)
    slack_len = jax.random.randint(key_slack, (pair_count,), 0, extra_room, dtype=jnp.int32)
    chosen = jax.random.randint(key_pick, (), 0, pair_count // pairs_each, dtype=jnp.int32)
    slack_len = jnp.where(pair_ids // pairs_each == chosen, 0, slack_len)
    first_len = jnp.where(pair_ids == chosen * pairs_each, MAXLEN, first_len)
    second = PAIRSUM - first_len - slack_len
    coin_flip = jax.random.randint(key_coin, (pair_count,), 0, 2, dtype=jnp.int32)
    left_len = jnp.where(coin_flip == 1, first_len, second)
    right_len = first_len + second - left_len
    slot_len = jnp.stack([left_len, right_len], axis=1).reshape(NSEQ)
    dealing = jax.random.permutation(key_order, NSEQ).astype(jnp.int32)
    lengths = jnp.zeros((NSEQ,), jnp.int32).at[dealing].set(slot_len)
    return (lengths, dealing)


def draw_lengths(key, part):
    return dealt_plan(key)[0]


def draw_dealing(key, part):
    return dealt_plan(key)[1]


def block_levels(stream_key, dims, shards, least, high):
    gain = 1.0
    for dim, shards_of in shards:
        steps = jax.random.uniform(jax.random.fold_in(jax.random.fold_in(stream_key, 6), dim), (shards_of,), jnp.float32, least / len(shards), high / len(shards))
        gain = gain * jnp.repeat(jnp.exp(steps), dims[dim] // shards_of).reshape((-1,) + (1,) * (len(dims) - 1 - dim))
    return gain


def bell_draw(own_key, dims, deviation, bound, shards=(), held_as=jnp.bfloat16):
    array = jax.random.normal(own_key, dims, jnp.float32) * deviation
    if len(shards) > 0:
        array = block_levels(own_key, dims, shards, -0.22, 0.18) * array
    return jnp.clip(array, min=-bound, max=bound).astype(held_as)


def setup_inputs(seed: int = 0) -> dict:
    streams_of = jax.random.split(jax.random.key(seed), 20)
    return {
        "tokens": bell_draw(streams_of[0], (NSEQ, MAXLEN, D), 1.0, 6.0, ((1, 32),)),
        "cotangent": bell_draw(streams_of[1], (PACKED, D), 1.0, 6.0, ((0, 32),)),
        "lengths": draw_lengths(jax.random.fold_in(streams_of[19], 71), 0),
        "dealing": draw_dealing(jax.random.fold_in(streams_of[19], 71), 0),
        "w_query": bell_draw(streams_of[4], (D, D), D ** -0.5, 0.21875, ((0, 32),)),
        "w_key": bell_draw(streams_of[5], (D, D), D ** -0.5, 0.21875, ((0, 32),)),
        "w_value": bell_draw(streams_of[6], (D, D), D ** -0.5, 0.21875, ((0, 32),)),
        "w_out": bell_draw(streams_of[7], (D, D), (D // 64) ** -0.5, 1.75, ((0, 32),)),
        "b_query": bell_draw(streams_of[8], (D,), 0.5, 3.0, ((0, 32),)),
        "b_value": bell_draw(streams_of[9], (D,), 0.5, 3.0, ((0, 32),)),
        "b_out": bell_draw(streams_of[10], (D,), 0.5, 3.0, ((0, 32),)),
        "norm1_gain": jnp.clip(1.0 + 0.1 * jax.random.normal(streams_of[11], (D,), jnp.float32), 0.5, 1.5).astype(jnp.bfloat16),
        "norm1_bias": bell_draw(streams_of[12], (D,), 0.5, 3.0, ((0, 32),)),
        "w_up": bell_draw(streams_of[13], (D, FF), D ** -0.5, 0.21875, ((0, 32),)),
        "b_up": bell_draw(streams_of[14], (FF,), 0.5, 3.0, ((0, 32),)),
        "w_down": bell_draw(streams_of[15], (FF, D), FF ** -0.5, 0.109375, ((0, 32),)),
        "b_down": bell_draw(streams_of[16], (D,), 0.5, 3.0, ((0, 32),)),
        "norm2_gain": jnp.clip(1.0 + 0.1 * jax.random.normal(streams_of[17], (D,), jnp.float32), 0.5, 1.5).astype(jnp.bfloat16),
        "norm2_bias": bell_draw(streams_of[18], (D,), 0.5, 3.0, ((0, 32),)),
    }


@jax.custom_vjp
def low(v):
    return lax.optimization_barrier(v.astype(jnp.bfloat16)).astype(jnp.float32)

@jax.custom_vjp
def low_back(v):
    return v

def low_keep(v):
    return (low(v), None)

def low_pass(kept, grad):
    return (grad,)

def back_keep(v):
    return (v, None)

def back_low(kept, grad):
    return (low(grad),)
low.defvjp(low_keep, low_pass)
low_back.defvjp(back_keep, back_low)
MASKED_SCORE = -1e+30
FULL_PRECISION = lax.Precision.HIGHEST

def matmul(left, right):
    return jnp.dot(left, right, precision=FULL_PRECISION, preferred_element_type=jnp.float32)

def layer_norm(residual, norm_gain, norm_shift):
    center = residual - lax.optimization_barrier(jnp.mean(residual, axis=-1, keepdims=True))
    scaled = center * lax.rsqrt(lax.optimization_barrier(jnp.mean(center * center, axis=-1, keepdims=True)) + 1e-05)
    return scaled * norm_gain + norm_shift

def group_layer(params, packed, segment, is_valid):
    w_query, w_key, w_value, w_out, b_query, b_value, b_out, norm1_gain, norm1_bias, w_up, b_up, w_down, b_down, norm2_gain, norm2_bias = params
    row_count = packed.shape[0]

    def by_head(matrix):
        return matrix.reshape(row_count, HEADS, HEAD_DIM)
    queries = low_back(low((matmul(packed, w_query) + b_query) * 0.125))
    key_rows = low_back(low(matmul(packed, w_key)))
    value_rows = low_back(low(matmul(packed, w_value) + b_value))
    same_segment = segment[:, None] == segment[None, :]
    scores = jnp.einsum('qhd,khd->hqk', by_head(queries), by_head(key_rows), precision=FULL_PRECISION)
    scores = jnp.where(same_segment[None], low_back(scores), MASKED_SCORE)
    log_total = jax.nn.logsumexp(scores, axis=-1, keepdims=True)
    attn_probs = low(jnp.exp(scores - log_total))
    context = jnp.einsum('hqk,khd->qhd', attn_probs, by_head(value_rows), precision=FULL_PRECISION)
    context = low_back(low(context.reshape(row_count, HEADS * HEAD_DIM)))
    attn_out = low_back(matmul(context, w_out) + b_out)
    hidden1 = layer_norm(packed + attn_out, norm1_gain, norm1_bias)
    pre_act = low_back(matmul(low(hidden1), w_up) + b_up)
    activated = low(jax.nn.gelu(pre_act, approximate=False))
    ffn_out = low_back(matmul(activated, w_down) + b_down)
    result = layer_norm(hidden1 + ffn_out, norm2_gain, norm2_bias)
    return jnp.where(is_valid[:, None], result, 0.0)

def reference(tokens, cotangent, lengths, dealing, w_query, w_key, w_value, w_out, b_query, b_value, b_out, norm1_gain, norm1_bias, w_up, b_up, w_down, b_down, norm2_gain, norm2_bias):
    params = tuple((weight.astype(jnp.float32) for weight in (w_query, w_key, w_value, w_out, b_query, b_value, b_out, norm1_gain, norm1_bias, w_up, b_up, w_down, b_down, norm2_gain, norm2_bias)))
    slot_len = jnp.take(lengths, dealing).reshape(N_DEV, SPD).astype(jnp.int32)
    slot_ends = jnp.cumsum(slot_len, axis=1).astype(jnp.int32)
    starts = (slot_ends - slot_len).astype(jnp.int32)
    row_ids = jnp.arange(CAP, dtype=jnp.int32)
    segment = lax.optimization_barrier(jnp.sum((row_ids[None, :, None] >= slot_ends[:, None, :]).astype(jnp.int32), axis=2)).astype(jnp.int32)
    is_valid = segment < SPD
    bounds = jnp.concatenate([starts, slot_ends[:, -1:]], axis=1).astype(jnp.int32)
    position = (row_ids[None, :] - jnp.take_along_axis(bounds, segment, axis=1)).astype(jnp.int32)
    owners = jnp.concatenate([dealing.reshape(N_DEV, SPD), jnp.zeros((N_DEV, 1), jnp.int32)], axis=1).astype(jnp.int32)
    owners = jnp.take_along_axis(owners, segment, axis=1)
    source = jnp.where(is_valid, owners * MAXLEN + position, 0).astype(jnp.int32)

    def forward(flat_tokens, weights):
        packed = jnp.where(is_valid[..., None], jnp.take(flat_tokens, source, axis=0), 0.0)

        def one_group(operands):
            return group_layer(weights, operands[0], operands[1], operands[2])
        return lax.map(jax.checkpoint(one_group), (packed, segment, is_valid))
    flat_tokens = tokens.astype(jnp.float32).reshape(NSEQ * MAXLEN, D)
    result, pullback = jax.vjp(forward, flat_tokens, params)
    grad_flat, grad_params = pullback(cotangent.astype(jnp.float32).reshape(N_DEV, CAP, D))
    return (result.reshape(N_DEV * CAP, D).astype(jnp.bfloat16), grad_flat.reshape(NSEQ, MAXLEN, D).astype(jnp.bfloat16), grad_params[0], grad_params[1], grad_params[2], grad_params[3], grad_params[4], grad_params[5], grad_params[6], grad_params[7], grad_params[8], grad_params[9], grad_params[10], grad_params[11], grad_params[12], grad_params[13], grad_params[14])
```

```python
from functools import partial

import jax
import jax.numpy as jnp
from jax import lax
from jax.experimental import pallas as pl
from jax.experimental.pallas import tpu as pltpu
from jax.sharding import PartitionSpec as P

HEADS = 12
HEAD_DIM = 64
PAIR = 2 * HEAD_DIM
GROUP = 4 * HEAD_DIM

MASKED_SCORE = -1e30
ROOT_HALF = 0.7071067811865476
INV_ROOT_TAU = 0.3989422804014327
BF16 = jnp.bfloat16
F32 = jnp.float32


def layer_norm(residual, norm_gain, norm_shift):
    center = residual - jnp.mean(residual, axis=-1, keepdims=True)
    inverse = lax.rsqrt(jnp.mean(center * center, axis=-1, keepdims=True) + 1e-05)
    normed = center * inverse
    return (normed * norm_gain + norm_shift, normed, inverse)


def norm_back(upstream, normed, inverse, norm_gain):
    scaled = upstream * norm_gain
    return inverse * (
        scaled
        - jnp.mean(scaled, axis=-1, keepdims=True)
        - normed * jnp.mean(scaled * normed, axis=-1, keepdims=True)
    )


def dot_nt(left, right):
    return lax.dot_general(left, right, (((1,), (1,)), ((), ())), preferred_element_type=F32)


def dot_nn(left, right):
    return lax.dot_general(left, right, (((1,), (0,)), ((), ())), preferred_element_type=F32)


def attention_forward_kernel(seg_col, seg_row, q_ref, k_ref, v_ref, ctx_ref, lse_ref, bias):
    step = pl.program_id(0)

    @pl.when(step == 0)
    def _():
        bias[...] = jnp.where(seg_col[...] == seg_row[...], 0.0, MASKED_SCORE)

    rows = q_ref.shape[0]
    lane = lax.broadcasted_iota(jnp.int32, (rows, PAIR), 1)
    stats = lse_ref[...]
    for pair in range(GROUP // PAIR):
        span = slice(pair * PAIR, (pair + 1) * PAIR)
        q_pair, k_pair, v_pair = q_ref[:, span], k_ref[:, span], v_ref[:, span]
        outs = []
        for half in range(2):
            own = (lane // HEAD_DIM) == half
            q_own = jnp.where(own, q_pair, jnp.zeros_like(q_pair))
            scores = dot_nt(q_own, k_pair) + bias[...]
            top = jnp.max(scores, axis=1, keepdims=True)
            weights = jnp.exp(scores - top)
            total = jnp.sum(weights, axis=1, keepdims=True)
            outs.append(dot_nn(weights.astype(BF16), v_pair) * (1.0 / total))
            head = step * (GROUP // HEAD_DIM) + pair * 2 + half
            stats = jnp.where(lane == head, top + jnp.log(total), stats)
        ctx_ref[:, span] = jnp.where(lane < HEAD_DIM, outs[0], outs[1]).astype(BF16)
    lse_ref[...] = stats


def attention_forward(segment, queries, key_rows, value_rows):
    rows, width = queries.shape
    block = pl.BlockSpec((rows, GROUP), lambda g: (0, g))
    whole = lambda shape: pl.BlockSpec(shape, lambda g: (0, 0))
    return pl.pallas_call(
        attention_forward_kernel,
        grid=(width // GROUP,),
        in_specs=[whole((rows, 1)), whole((1, rows)), block, block, block],
        out_specs=[block, whole((rows, PAIR))],
        out_shape=[
            jax.ShapeDtypeStruct((rows, width), BF16),
            jax.ShapeDtypeStruct((rows, PAIR), F32),
        ],
        scratch_shapes=[pltpu.VMEM((rows, rows), F32)],
        compiler_params=pltpu.CompilerParams(vmem_limit_bytes=48 << 20),
        cost_estimate=pl.CostEstimate(
            flops=HEADS * rows * rows * PAIR * 4,
            transcendentals=HEADS * rows * rows,
            bytes_accessed=rows * width * 8,
        ),
    )(segment[:, None], segment[None, :], queries, key_rows, value_rows)


def attention_backward_kernel(
    seg_col, seg_row, lse_ref, q_ref, k_ref, v_ref, g_ref, dq_ref, dk_ref, dv_ref, bias
):
    step = pl.program_id(0)

    @pl.when(step == 0)
    def _():
        bias[...] = jnp.where(seg_col[...] == seg_row[...], 0.0, MASKED_SCORE)

    rows = q_ref.shape[0]
    lane = lax.broadcasted_iota(jnp.int32, (rows, PAIR), 1)
    for pair in range(GROUP // PAIR):
        span = slice(pair * PAIR, (pair + 1) * PAIR)
        q_pair, k_pair, v_pair, g_pair = (
            q_ref[:, span],
            k_ref[:, span],
            v_ref[:, span],
            g_ref[:, span],
        )
        q_turn, g_turn = q_pair.T, g_pair.T
        dq, dk, dv = [], [], []
        for half in range(2):
            own = (lane // HEAD_DIM) == half
            part = slice(half * HEAD_DIM, (half + 1) * HEAD_DIM)
            zero = jnp.zeros_like(q_pair)
            head = step * (GROUP // HEAD_DIM) + pair * 2 + half
            log_total = jnp.sum(jnp.where(lane == head, lse_ref[...], 0.0), axis=1, keepdims=True)
            scores = dot_nt(jnp.where(own, q_pair, zero), k_pair) + bias[...]
            probs = jnp.exp(scores - log_total)
            low = probs.astype(BF16)
            g_probs = dot_nt(jnp.where(own, g_pair, zero), v_pair)
            product = probs * g_probs
            g_scores = (product - probs * jnp.sum(product, axis=1, keepdims=True)).astype(BF16)
            dq.append(dot_nn(g_scores, k_pair))
            dk.append(dot_nn(q_turn[part], g_scores))
            dv.append(dot_nn(g_turn[part], low))
        dq_ref[:, span] = jnp.where(lane < HEAD_DIM, dq[0], dq[1]).astype(BF16)
        dk_ref[:, span] = jnp.concatenate(dk, axis=0).T.astype(BF16)
        dv_ref[:, span] = jnp.concatenate(dv, axis=0).T.astype(BF16)


def attention_backward(segment, log_total, queries, key_rows, value_rows, g_context):
    rows, width = queries.shape
    block = pl.BlockSpec((rows, GROUP), lambda g: (0, g))
    whole = lambda shape: pl.BlockSpec(shape, lambda g: (0, 0))
    return pl.pallas_call(
        attention_backward_kernel,
        grid=(width // GROUP,),
        in_specs=[whole((rows, 1)), whole((1, rows)), whole((rows, PAIR))] + [block] * 4,
        out_specs=[block] * 3,
        out_shape=[jax.ShapeDtypeStruct((rows, width), BF16)] * 3,
        scratch_shapes=[pltpu.VMEM((rows, rows), F32)],
        compiler_params=pltpu.CompilerParams(vmem_limit_bytes=48 << 20),
        cost_estimate=pl.CostEstimate(
            flops=HEADS * rows * rows * PAIR * 10,
            transcendentals=HEADS * rows * rows,
            bytes_accessed=rows * width * 14,
        ),
    )(segment[:, None], segment[None, :], log_total, queries, key_rows, value_rows, g_context)


def flip(array, stride):
    devices = lax.axis_size("dev")
    return lax.ppermute(array, "dev", [(i, i ^ stride) for i in range(devices)])


def far_groups():
    devices = lax.axis_size("dev")
    return [[near + 8 * far for far in range(devices // 8)] for near in range(8)]


def bit(stride):
    return (lax.axis_index("dev") // stride) % 2


def halves(array, axis, stride):
    mine = bit(stride)
    keep = lax.dynamic_index_in_dim(array, mine, axis, keepdims=False)
    send = lax.dynamic_index_in_dim(array, 1 - mine, axis, keepdims=False)
    return keep, send


def joined(mine, theirs, stride):
    low = bit(stride) == 0
    return jnp.stack([jnp.where(low, mine, theirs), jnp.where(low, theirs, mine)])


def gather_far(shard):
    far = lax.axis_size("dev") // 8
    spread = jnp.broadcast_to(shard[None], (far,) + shard.shape)
    return lax.all_to_all(spread, "dev", 0, 0, axis_index_groups=far_groups())


def gather_near(block, first, second):
    block = joined(block, flip(block, first), first)
    block = joined(block, flip(block, second), second)
    block = joined(block, flip(block, 1), 1)
    order = (3, 1, 2, 0) if second == 4 else (3, 2, 1, 0)
    rest = tuple(range(4, block.ndim))
    block = block.transpose(order + rest)
    return block.reshape((block.shape[0] * 8,) + block.shape[4:])


def add_low(left, right):
    return (left.astype(F32) + right.astype(F32)).astype(BF16)


def scatter_near(grads, first, second):
    far = grads.shape[0] // 8
    part = grads.reshape((far, 2, 2, 2) + grads.shape[1:])
    keep, send = halves(part, 3, 1)
    part = add_low(keep, flip(send, 1))
    keep, send = halves(part, 2 if first == 2 else 1, first)
    part = add_low(keep, flip(send, first))
    keep, send = halves(part, 1, second)
    return add_low(keep, flip(send, second))


def scatter_far(part):
    got = lax.all_to_all(part, "dev", 0, 0, axis_index_groups=far_groups())
    return jnp.sum(got.astype(F32), axis=0)


def padded_rows(array, rows, width):
    flat = array.reshape(array.shape[0], -1)
    flat = jnp.pad(flat, ((0, 0), (0, width - flat.shape[1])))
    return jnp.pad(flat[:, None], ((0, 0), (0, rows - 1), (0, 0)))


def shards(
    tokens,
    cotangent,
    lengths,
    dealing,
    w_query,
    w_key,
    w_value,
    w_out,
    b_query,
    b_value,
    b_out,
    norm1_gain,
    norm1_bias,
    w_up,
    b_up,
    w_down,
    b_down,
    norm2_gain,
    norm2_bias,
):
    devices = lax.axis_size("dev")
    me = lax.axis_index("dev")
    seq_count, local_len, width = tokens.shape
    per_device = seq_count // devices
    longest = local_len * devices
    capacity = cotangent.shape[0]
    share = w_query.shape[0]
    hidden = w_up.shape[1]

    outgoing = jnp.take(tokens, dealing, axis=0).reshape(devices, per_device, local_len, width)
    arrived = lax.all_to_all(outgoing, "dev", 0, 0)

    vectors = (
        b_query,
        b_value,
        b_out,
        norm1_gain,
        norm1_bias,
        b_down,
        norm2_gain,
        norm2_bias,
        b_up,
    )
    vector_row = padded_rows(jnp.concatenate(vectors)[None], 8, width)[0]
    attn_far_a = gather_far(jnp.concatenate([w_query, w_key], axis=0))
    attn_far_b = gather_far(jnp.concatenate([w_value, w_out, vector_row], axis=0))
    attn_a = gather_near(attn_far_a, 2, 4)
    attn_b = gather_near(attn_far_b, 4, 2)
    full_wq = attn_a[:, :share].reshape(width, width)
    full_wk = attn_a[:, share:].reshape(width, width)
    full_wv = attn_b[:, :share].reshape(width, width)
    full_wo = attn_b[:, share : 2 * share].reshape(width, width)
    full_vec = attn_b[:, 2 * share, : 8 * share + hidden // devices].astype(F32)
    full_bq, full_bv, full_bo, gain_one, shift_one, full_bdown, gain_two, shift_two = (
        full_vec[:, i * share : (i + 1) * share].reshape(width) for i in range(8)
    )
    full_bup = full_vec[:, 8 * share :].reshape(hidden)

    up_far = gather_far(w_up)
    down_far = gather_far(w_down)
    full_up = gather_near(up_far, 2, 4).reshape(width, hidden)
    full_down = gather_near(down_far, 4, 2).reshape(hidden, width)

    my_slots = lax.dynamic_slice_in_dim(dealing, me * per_device, per_device)
    slot_len = jnp.take(lengths, my_slots)
    slot_ends = jnp.cumsum(slot_len)
    starts = slot_ends - slot_len
    row_ids = jnp.arange(capacity, dtype=jnp.int32)
    segment = jnp.sum((row_ids[:, None] >= slot_ends[None, :]).astype(jnp.int32), axis=1)
    is_valid = segment < per_device
    bounds = jnp.concatenate([starts, slot_ends[-1:]])
    picked = segment[:, None] == jnp.arange(per_device + 1, dtype=jnp.int32)[None, :]
    position = row_ids - jnp.sum(jnp.where(picked, bounds[None, :], 0), axis=1)
    source = (position // local_len) * (per_device * local_len) + segment * local_len
    source = jnp.where(is_valid, source + position % local_len, 0)
    packed = jnp.where(
        is_valid[:, None],
        jnp.take(arrived.reshape(-1, width), source, axis=0),
        jnp.zeros((), BF16),
    )

    queries = ((jnp.dot(packed, full_wq, preferred_element_type=F32) + full_bq) * 0.125).astype(
        BF16
    )
    key_rows = jnp.dot(packed, full_wk, preferred_element_type=F32).astype(BF16)
    value_rows = (jnp.dot(packed, full_wv, preferred_element_type=F32) + full_bv).astype(BF16)
    context, log_total = attention_forward(segment, queries, key_rows, value_rows)
    attn_out = jnp.dot(context, full_wo, preferred_element_type=F32) + full_bo
    hidden1, normed1, inverse1 = layer_norm(packed.astype(F32) + attn_out, gain_one, shift_one)
    hidden1_low = hidden1.astype(BF16)
    pre_act = jnp.dot(hidden1_low, full_up, preferred_element_type=F32) + full_bup
    activated = jax.nn.gelu(pre_act, approximate=False).astype(BF16)
    ffn_out = jnp.dot(activated, full_down, preferred_element_type=F32) + full_bdown
    result, normed2, inverse2 = layer_norm(hidden1 + ffn_out, gain_two, shift_two)
    layer_out = jnp.where(is_valid[:, None], result, 0.0).astype(BF16)

    g_out = cotangent.astype(F32) * is_valid[:, None].astype(F32)
    g_gain_two = jnp.sum(g_out * normed2, axis=0)
    g_shift_two = jnp.sum(g_out, axis=0)
    g_resid2 = norm_back(g_out, normed2, inverse2, gain_two)
    g_ffn = g_resid2.astype(BF16)
    g_bdown = jnp.sum(g_ffn, axis=0, dtype=F32)
    g_down = jnp.dot(activated.T, g_ffn, preferred_element_type=F32).astype(BF16)
    down_part = scatter_near(g_down.reshape(devices, hidden // devices, width), 2, 4)
    g_act = jnp.dot(g_ffn, full_down.T, preferred_element_type=F32)
    gelu_slope = (
        0.5 * (1.0 + lax.erf(pre_act * ROOT_HALF))
        + pre_act * jnp.exp(-0.5 * pre_act * pre_act) * INV_ROOT_TAU
    )
    g_pre = (g_act * gelu_slope).astype(BF16)
    g_bup = jnp.sum(g_pre, axis=0, dtype=F32)
    g_up = jnp.dot(hidden1_low.T, g_pre, preferred_element_type=F32).astype(BF16)
    up_part = scatter_near(g_up.reshape(devices, share, hidden), 4, 2)
    g_wdown = scatter_far(down_part)
    g_wup = scatter_far(up_part)

    g_hidden1 = jnp.dot(g_pre, full_up.T, preferred_element_type=F32) + g_resid2
    g_gain_one = jnp.sum(g_hidden1 * normed1, axis=0)
    g_shift_one = jnp.sum(g_hidden1, axis=0)
    g_resid1 = norm_back(g_hidden1, normed1, inverse1, gain_one)
    g_attn = g_resid1.astype(BF16)
    g_bo = jnp.sum(g_attn, axis=0, dtype=F32)
    g_context = jnp.dot(g_attn, full_wo.T, preferred_element_type=F32).astype(BF16)
    g_queries, g_keys, g_values = attention_backward(
        segment, log_total, queries, key_rows, value_rows, g_context
    )
    g_bq = jnp.sum(g_queries, axis=0, dtype=F32) * 0.125
    g_bv = jnp.sum(g_values, axis=0, dtype=F32)
    g_input = (
        jnp.dot(g_queries, full_wq.T, preferred_element_type=F32) * 0.125
        + jnp.dot(g_keys, full_wk.T, preferred_element_type=F32)
        + jnp.dot(g_values, full_wv.T, preferred_element_type=F32)
        + g_resid1
    ).astype(BF16)

    step_ids = jnp.arange(longest, dtype=jnp.int32).reshape(devices, 1, local_len)
    inside = step_ids < slot_len[None, :, None]
    take_rows = jnp.where(inside, starts[None, :, None] + step_ids, 0)
    unpacked = jnp.where(
        inside[..., None], jnp.take(g_input, take_rows, axis=0), jnp.zeros((), BF16)
    )
    returned = lax.all_to_all(unpacked, "dev", 0, 0)
    slots = jnp.arange(seq_count, dtype=jnp.int32)
    inverse_deal = jnp.sum(jnp.where(dealing[None, :] == slots[:, None], slots[None, :], 0), axis=1)
    input_grad = jnp.take(returned.reshape(seq_count, local_len, width), inverse_deal, axis=0)

    g_wq = (jnp.dot(packed.T, g_queries, preferred_element_type=F32) * 0.125).astype(BF16)
    g_wk = jnp.dot(packed.T, g_keys, preferred_element_type=F32).astype(BF16)
    g_wv = jnp.dot(packed.T, g_values, preferred_element_type=F32).astype(BF16)
    g_wo = jnp.dot(context.T, g_attn, preferred_element_type=F32).astype(BF16)
    g_vectors = (
        g_bq,
        g_bv,
        g_bo,
        g_gain_one,
        g_shift_one,
        g_bdown,
        g_gain_two,
        g_shift_two,
        g_bup,
    )
    g_vec = jnp.concatenate([v.reshape(devices, -1) for v in g_vectors], axis=1).astype(BF16)
    g_vec = padded_rows(g_vec, 8, width)

    def dealt(matrix):
        return matrix.reshape(devices, share, width)

    attn_part_a = scatter_near(jnp.concatenate([dealt(g_wq), dealt(g_wk)], axis=1), 2, 4)
    attn_part_b = scatter_near(jnp.concatenate([dealt(g_wv), dealt(g_wo), g_vec], axis=1), 4, 2)
    attn_a = scatter_far(attn_part_a)
    attn_b = scatter_far(attn_part_b)
    own_vec = attn_b[2 * share]
    small = [own_vec[i * share : (i + 1) * share] for i in range(8)]
    g_bup_own = own_vec[8 * share : 8 * share + hidden // devices]
    return (
        layer_out,
        input_grad,
        attn_a[:share],
        attn_a[share:],
        attn_b[:share],
        attn_b[share : 2 * share],
        small[0],
        small[1],
        small[2],
        small[3],
        small[4],
        g_wup,
        g_bup_own,
        g_wdown,
        small[5],
        small[6],
        small[7],
    )


def solution(mesh):
    rows = P("dev", None)
    vector = P("dev")
    seqs = P(None, "dev", None)
    return jax.shard_map(
        shards,
        mesh=mesh,
        in_specs=(
            (seqs, rows, P(), P())
            + (rows,) * 4
            + (vector,) * 5
            + (rows, vector, rows)
            + (vector,) * 3
        ),
        out_specs=(
            (rows, seqs) + (rows,) * 4 + (vector,) * 5 + (rows, vector, rows) + (vector,) * 3
        ),
        check_vma=False,
    )
```

```python
from functools import partial

import jax
import jax.numpy as jnp
from jax import lax
from jax.experimental import pallas as pl
from jax.experimental.pallas import tpu as pltpu
from jax.sharding import PartitionSpec as P

HEADS = 12
HEAD_DIM = 64
PAIR = 2 * HEAD_DIM
GROUP = 4 * HEAD_DIM

MASKED_SCORE = -1e30
ROOT_HALF = 0.7071067811865476
INV_ROOT_TAU = 0.3989422804014327
BF16 = jnp.bfloat16
F32 = jnp.float32


def layer_norm(residual, norm_gain, norm_shift):
    center = residual - jnp.mean(residual, axis=-1, keepdims=True)
    inverse = lax.rsqrt(jnp.mean(center * center, axis=-1, keepdims=True) + 1e-05)
    normed = center * inverse
    return (normed * norm_gain + norm_shift, normed, inverse)


def norm_back(upstream, normed, inverse, norm_gain):
    scaled = upstream * norm_gain
    return inverse * (
        scaled
        - jnp.mean(scaled, axis=-1, keepdims=True)
        - normed * jnp.mean(scaled * normed, axis=-1, keepdims=True)
    )


def dot_nt(left, right):
    return lax.dot_general(left, right, (((1,), (1,)), ((), ())), preferred_element_type=F32)


def dot_nn(left, right):
    return lax.dot_general(left, right, (((1,), (0,)), ((), ())), preferred_element_type=F32)


def piece_blocks(devices, height, split):
    for core in range(2):
        for far in range(devices // 8):
            for near in range(4):
                relative = core + 2 * near + 8 * far
                if near < 3:
                    yield 5 * core + near, far, relative, 0, height
                else:
                    yield 5 * core + 3, far, relative, 0, split
                    yield 5 * core + 4, far, relative, split, height


def all_done(ref, sem):
    pltpu.make_async_copy(ref, ref, sem).wait()


def prepare_kernel(me_ref, *refs):
    weights, up_ref, down_ref, vectors, b_up = refs[:4], refs[4], refs[5], refs[6:14], refs[14]
    attn_ref, ffn_ref, rows_ref = refs[15:]
    share, width = weights[0].shape
    long = b_up.shape[1]
    me = me_ref[0]
    for i, weight in enumerate(weights):
        attn_ref[i * share : (i + 1) * share] = weight[...]
    ffn_ref[:long] = down_ref[...]
    for b in range(long // share):
        row = long + b * share
        ffn_ref[row : row + share] = up_ref[:, b * width : (b + 1) * width]
    rows_ref[...] = jnp.zeros_like(rows_ref)
    for i, vector in enumerate(vectors):
        rows_ref[i : i + 1, 0:share] = vector[...].astype(F32)
    for i in range(8, 16):
        rows_ref[i : i + 1, 0:long] = b_up[...].astype(F32)
    values = rows_ref[...].astype(BF16)
    shape = (values.shape[1], width)
    source = lax.broadcasted_iota(jnp.int32, shape, 0)
    target = lax.broadcasted_iota(jnp.int32, shape, 1)
    moved = []
    for start in (me * share, (me * long) % width):
        here = jnp.where(target == source + start, 1.0, 0.0).astype(BF16)
        moved.append(dot_nn(values, here))
    row = lax.broadcasted_iota(jnp.int32, moved[0].shape, 0)
    of_up = jnp.where(row == 8 + (me * long) // width, moved[1], 0.0)
    attn_ref[4 * share :] = jnp.where(row < 8, moved[0], of_up).astype(BF16)


def prepare(me, weights, w_up, w_down, vectors, b_up):
    share, width = weights[0].shape
    long = w_down.shape[0]
    vmem = pl.BlockSpec(memory_space=pltpu.VMEM)
    smem = pl.BlockSpec(memory_space=pltpu.SMEM)
    rows = [vector.reshape(1, -1) for vector in vectors + (b_up,)]
    return pl.pallas_call(
        prepare_kernel,
        in_specs=[smem] + [vmem] * 15,
        out_specs=[vmem] * 2,
        out_shape=[
            jax.ShapeDtypeStruct((4 * share + 16, width), BF16),
            jax.ShapeDtypeStruct((2 * long, width), BF16),
        ],
        scratch_shapes=[pltpu.VMEM((16, PAIR), F32)],
        cost_estimate=pl.CostEstimate(flops=1 << 22, transcendentals=0, bytes_accessed=1 << 20),
    )(me, *weights, w_up, w_down, *rows)


def attention_forward_kernel(
    blocked,
    devices,
    me_ref,
    seg_col,
    seg_row,
    source_ref,
    arrived_ref,
    *refs,
):
    pieces, refs = (refs[:10], refs[10:]) if blocked else (refs[:2], refs[2:])
    packed_ref, q_ref, k_ref, v_ref, ctx_ref, lse_ref, resid_ref, vec_ref, w_out_ref = refs[:9]
    weights, vec_rows, bias, sems = refs[9:]
    step = pl.program_id(0)
    rows, width = packed_ref.shape
    share = width // devices
    me = me_ref[0]

    @pl.when(step == 0)
    def _():
        if blocked:
            height = 4 * share + 16
            for array, far, relative, top, bottom in piece_blocks(devices, height, 2 * share):
                row = pl.multiple_of((relative ^ me) * share, 8)
                for i in range(top // share, min(bottom // share, 4)):
                    pltpu.make_async_copy(
                        pieces[array].at[far, pl.ds(i * share - top, share)],
                        weights.at[i, pl.ds(row, share)],
                        sems.at[0],
                    ).start()
                if bottom == height:
                    pltpu.make_async_copy(
                        pieces[array].at[far, pl.ds(4 * share - top, 16)],
                        vec_rows.at[relative],
                        sems.at[1],
                    ).start()
        else:
            pltpu.make_async_copy(pieces[0], weights, sems.at[0]).start()
            pltpu.make_async_copy(pieces[1], vec_rows, sems.at[1]).start()
        bias[...] = jnp.where(seg_col[...] == seg_row[...], 0.0, MASKED_SCORE)
        places = arrived_ref.shape[0]
        block = rows // 4
        for i in range(4):
            here = slice(i * block, (i + 1) * block)
            pick = source_ref[here] == lax.broadcasted_iota(jnp.int32, (block, places), 1)
            pick = jnp.where(pick, 1.0, 0.0).astype(BF16)
            packed_ref[here] = dot_nn(pick, arrived_ref[...]).astype(BF16)
        all_done(vec_rows, sems.at[1])
        all_done(weights, sems.at[0])
        vec_ref[...] = jnp.sum(vec_rows[...].astype(F32), axis=0)
        resid_ref[...] = packed_ref[...].astype(F32) + vec_ref[2:3, :]
        pltpu.make_async_copy(weights, w_out_ref, sems.at[2]).start()

    packed = packed_ref[...]
    group = pl.ds(pl.multiple_of(step * GROUP, GROUP), GROUP)
    q_ref[...] = ((dot_nn(packed, weights[0, :, group]) + vec_ref[0:1, group]) * 0.125).astype(BF16)
    k_ref[...] = dot_nn(packed, weights[1, :, group]).astype(BF16)
    v_ref[...] = (dot_nn(packed, weights[2, :, group]) + vec_ref[1:2, group]).astype(BF16)
    lane = lax.broadcasted_iota(jnp.int32, (rows, PAIR), 1)
    stats = lse_ref[...]
    for pair in range(GROUP // PAIR):
        span = slice(pair * PAIR, (pair + 1) * PAIR)
        q_pair, k_pair, v_pair = q_ref[:, span], k_ref[:, span], v_ref[:, span]
        outs = []
        for half in range(2):
            own = (lane // HEAD_DIM) == half
            q_own = jnp.where(own, q_pair, jnp.zeros_like(q_pair))
            scores = dot_nt(q_own, k_pair) + bias[...]
            top = jnp.max(scores, axis=1, keepdims=True)
            exped = jnp.exp(scores - top)
            total = jnp.sum(exped, axis=1, keepdims=True)
            outs.append(dot_nn(exped.astype(BF16), v_pair) * (1.0 / total))
            head = step * (GROUP // HEAD_DIM) + pair * 2 + half
            stats = jnp.where(lane == head, top + jnp.log(total), stats)
        ctx_ref[:, span] = jnp.where(lane < HEAD_DIM, outs[0], outs[1]).astype(BF16)
    lse_ref[...] = stats
    resid_ref[...] += dot_nn(ctx_ref[...], weights[3, group, :])

    @pl.when(step == pl.num_programs(0) - 1)
    def _():
        pltpu.make_async_copy(weights, w_out_ref, sems.at[2]).wait()


def natural(pieces):
    corners = [jnp.concatenate(pieces[i + 3 : i + 5], axis=1) for i in (0, 5)]
    blocks = jnp.stack(
        [b for i, corner in zip((0, 5), corners) for b in (*pieces[i : i + 3], corner)], axis=1
    )
    far = blocks.shape[0]
    blocks = blocks.reshape((far, 2, 4) + blocks.shape[2:]).swapaxes(1, 2)
    return in_order(blocks.reshape((8 * far,) + blocks.shape[3:]))


def attention_forward(me, devices, segment, source, arrived, pieces):
    rows, width = segment.shape[0], arrived.shape[1]
    share = width // devices
    blocked = share % 8 == 0
    if not blocked:
        rows_of = natural(pieces)
        parts = [rows_of[:, i * share : (i + 1) * share].reshape(width, width) for i in range(4)]
        pieces = (jnp.stack(parts), rows_of[:, 4 * share :])
    block = pl.BlockSpec((rows, GROUP), lambda g: (0, g))
    whole = lambda shape: pl.BlockSpec(shape, lambda g: (0, 0))
    any_space = pl.BlockSpec(memory_space=pl.ANY)
    return pl.pallas_call(
        partial(attention_forward_kernel, blocked, devices),
        grid=(width // GROUP,),
        in_specs=[
            pl.BlockSpec(memory_space=pltpu.SMEM),
            whole((rows, 1)),
            whole((1, rows)),
            whole((rows, 1)),
            whole(arrived.shape),
        ]
        + [any_space] * len(pieces),
        out_specs=[
            whole((rows, width)),
            block,
            block,
            block,
            block,
            whole((rows, PAIR)),
            whole((rows, width)),
            whole((16, width)),
            any_space,
        ],
        out_shape=[jax.ShapeDtypeStruct((rows, width), BF16)] * 5
        + [
            jax.ShapeDtypeStruct((rows, PAIR), F32),
            jax.ShapeDtypeStruct((rows, width), F32),
            jax.ShapeDtypeStruct((16, width), F32),
            jax.ShapeDtypeStruct((4, width, width), BF16),
        ],
        scratch_shapes=[
            pltpu.VMEM((4, width, width), BF16),
            pltpu.VMEM((devices, 16, width), BF16),
            pltpu.VMEM((rows, rows), F32),
            pltpu.SemaphoreType.DMA((3,)),
        ],
        compiler_params=pltpu.CompilerParams(vmem_limit_bytes=56 << 20),
        cost_estimate=pl.CostEstimate(
            flops=HEADS * rows * rows * PAIR * 4 + 8 * rows * width * width,
            transcendentals=HEADS * rows * rows,
            bytes_accessed=16 * width * width + rows * width * 18,
        ),
    )(me, segment[:, None], segment[None, :], source[:, None], arrived, *pieces)


def attention_backward_kernel(
    first,
    seg_col,
    seg_row,
    lse_ref,
    g_attn_ref,
    w_out_ref,
    q_ref,
    k_ref,
    v_ref,
    dq_ref,
    dk_ref,
    dv_ref,
    bias,
):
    step = pl.program_id(0)

    @pl.when(step == 0)
    def _():
        bias[...] = jnp.where(seg_col[...] == seg_row[...], 0.0, MASKED_SCORE)

    rows = q_ref.shape[0]
    lane = lax.broadcasted_iota(jnp.int32, (rows, PAIR), 1)
    g_context = dot_nt(g_attn_ref[...], w_out_ref[...]).astype(BF16)
    for pair in range(GROUP // PAIR):
        span = slice(pair * PAIR, (pair + 1) * PAIR)
        q_pair, k_pair, v_pair = q_ref[:, span], k_ref[:, span], v_ref[:, span]
        g_pair = g_context[:, span]
        q_turn, g_turn = q_pair.T, g_pair.T
        dq, dk, dv = [], [], []
        for half in range(2):
            own = (lane // HEAD_DIM) == half
            part = slice(half * HEAD_DIM, (half + 1) * HEAD_DIM)
            zero = jnp.zeros_like(q_pair)
            head = (first + step) * (GROUP // HEAD_DIM) + pair * 2 + half
            log_total = jnp.sum(jnp.where(lane == head, lse_ref[...], 0.0), axis=1, keepdims=True)
            scores = dot_nt(jnp.where(own, q_pair, zero), k_pair) + bias[...]
            probs = jnp.exp(scores - log_total)
            low = probs.astype(BF16)
            g_probs = dot_nt(jnp.where(own, g_pair, zero), v_pair)
            product = probs * g_probs
            g_scores = (product - probs * jnp.sum(product, axis=1, keepdims=True)).astype(BF16)
            dq.append(dot_nn(g_scores, k_pair))
            dk.append(dot_nn(q_turn[part], g_scores))
            dv.append(dot_nn(g_turn[part], low))
        dq_ref[:, span] = jnp.where(lane < HEAD_DIM, dq[0], dq[1]).astype(BF16)
        dk_ref[:, span] = jnp.concatenate(dk, axis=0).T.astype(BF16)
        dv_ref[:, span] = jnp.concatenate(dv, axis=0).T.astype(BF16)


def attention_backward(first, last, segment, log_total, g_attn, weights, queries, key_rows, value_rows):
    rows, width = queries.shape
    taken = pl.BlockSpec((rows, GROUP), lambda g: (0, g + first))
    made = pl.BlockSpec((rows, GROUP), lambda g: (0, g))
    whole = lambda shape: pl.BlockSpec(shape, lambda g: (0, 0))
    count = last - first
    return pl.pallas_call(
        partial(attention_backward_kernel, first),
        grid=(count,),
        in_specs=[
            whole((rows, 1)),
            whole((1, rows)),
            whole((rows, PAIR)),
            whole((rows, width)),
            pl.BlockSpec((None, GROUP, width), lambda g: (3, g + first, 0)),
        ]
        + [taken] * 3,
        out_specs=[made] * 3,
        out_shape=[jax.ShapeDtypeStruct((rows, count * GROUP), BF16)] * 3,
        scratch_shapes=[pltpu.VMEM((rows, rows), F32)],
        compiler_params=pltpu.CompilerParams(vmem_limit_bytes=48 << 20),
        cost_estimate=pl.CostEstimate(
            flops=count * 4 * rows * rows * PAIR * 10,
            transcendentals=count * 4 * rows * rows,
            bytes_accessed=count * rows * GROUP * 14,
        ),
    )(segment[:, None], segment[None, :], log_total, g_attn, weights, queries, key_rows, value_rows)


def input_gradient_kernel(parts, row_ref, resid_ref, w_ref, *refs):
    out_ref = refs[-1]
    rows = resid_ref.shape[0]
    total = resid_ref[...]
    column = 0
    for i in range(parts):
        dq, dk, dv = (refs[3 * i + j] for j in range(3))
        span = slice(column, column + dq.shape[1])
        column += dq.shape[1]
        total += dot_nt(dq[...], w_ref[0, :, span]) * 0.125
        total += dot_nt(dk[...], w_ref[1, :, span])
        total += dot_nt(dv[...], w_ref[2, :, span])
    g_input = total.astype(BF16)
    places = row_ref.shape[0]
    block = places // 4
    for i in range(4):
        here = slice(i * block, (i + 1) * block)
        pick = row_ref[here] == lax.broadcasted_iota(jnp.int32, (block, rows), 1)
        pick = jnp.where(pick, 1.0, 0.0).astype(BF16)
        out_ref[here] = dot_nn(pick, g_input).astype(BF16)


def input_gradient(take_rows, g_resid1, weights, gradients):
    rows, width = g_resid1.shape
    places = take_rows.shape[0]
    flat = [g for group in gradients for g in group]
    vmem = pl.BlockSpec(memory_space=pltpu.VMEM)
    return pl.pallas_call(
        partial(input_gradient_kernel, len(gradients)),
        in_specs=[vmem] * (3 + len(flat)),
        out_specs=vmem,
        out_shape=jax.ShapeDtypeStruct((places, width), BF16),
        compiler_params=pltpu.CompilerParams(vmem_limit_bytes=48 << 20),
        cost_estimate=pl.CostEstimate(
            flops=6 * rows * width * width + 2 * places * rows * width,
            transcendentals=0,
            bytes_accessed=12 * width * width + 10 * rows * width + 2 * places * width,
        ),
    )(take_rows[:, None], g_resid1, weights, *flat)


def paired_store(values, index, core, keep_ref, send_ref):
    low, high = values
    first = core == 0
    keep_ref[index] = jnp.where(first, low, high)
    send_ref[index] = jnp.where(first, high, low)


def weight_gradient_kernel(blocked, parts, me_ref, x_ref, ctx_ref, g_attn_ref, *refs):
    ins, outs = refs[: 3 * parts], refs[3 * parts :]
    rows, width = x_ref.shape
    me = me_ref[0]
    core = me & 1
    vec_ref = outs[-1]
    vec_ref[...] = jnp.zeros_like(vec_ref)

    def store(kind, grad):
        if not blocked:
            outs[0][kind] = grad
            return
        keep, send = (outs[2 * (kind // 2) + i] for i in range(2))
        share = keep.shape[2]
        for i in range(keep.shape[0]):
            low, high = (grad[(2 * i + j) * share : (2 * i + j + 1) * share] for j in range(2))
            paired_store((low, high), (i ^ (me >> 1), kind % 2), core, keep, send)

    x_turn = x_ref[...].T
    for j in range(3):
        pieces = []
        for i in range(parts):
            grads = ins[3 * i + j][...]
            span = slice(i * grads.shape[1], (i + 1) * grads.shape[1])
            piece = dot_nn(x_turn, grads)
            pieces.append((piece * 0.125 if j == 0 else piece).astype(BF16))
        store(j, jnp.concatenate(pieces, axis=1))
    store(3, dot_tn(ctx_ref[...], g_attn_ref[...]).astype(BF16))
    column = 0
    for i in range(parts):
        dq, _, dv = (ins[3 * i + j][...].astype(F32) for j in range(3))
        span = slice(column, column + dq.shape[1])
        column += dq.shape[1]
        vec_ref[0:1, span] = jnp.sum(dq, axis=0, keepdims=True) * 0.125
        vec_ref[1:2, span] = jnp.sum(dv, axis=0, keepdims=True)


def weight_gradients(me, devices, packed, context, g_attn, gradients):
    rows, width = packed.shape
    share = width // devices
    blocked = share % 8 == 0
    flat = [g for group in gradients for g in group]
    vmem = pl.BlockSpec(memory_space=pltpu.VMEM)
    smem = pl.BlockSpec(memory_space=pltpu.SMEM)
    if blocked:
        shapes = [jax.ShapeDtypeStruct((devices // 2, 2, share, width), BF16)] * 4
    else:
        shapes = [jax.ShapeDtypeStruct((4, width, width), BF16)]
    shapes.append(jax.ShapeDtypeStruct((8, width), F32))
    outs = pl.pallas_call(
        partial(weight_gradient_kernel, blocked, len(gradients)),
        in_specs=[smem] + [vmem] * (3 + len(flat)),
        out_specs=[vmem] * len(shapes),
        out_shape=shapes,
        compiler_params=pltpu.CompilerParams(vmem_limit_bytes=48 << 20),
        cost_estimate=pl.CostEstimate(
            flops=8 * rows * width * width,
            transcendentals=0,
            bytes_accessed=8 * width * width + 12 * rows * width,
        ),
    )(me, packed, context, g_attn, *flat)
    if blocked:
        return outs
    grads = in_order(outs[0].reshape(4, devices, share, width).transpose(1, 0, 2, 3))
    grads = grads.reshape(devices // 2, 2, 4, share, width)
    return [grads[:, i, j : j + 2] for j in (0, 2) for i in range(2)] + [outs[1]]


def dot_tn(left, right):
    return lax.dot_general(left, right, (((0,), (0,)), ((), ())), preferred_element_type=F32)


def feed_forward_kernel(blocked, devices, me_ref, count_ref, resid1_ref, cot_ref, vec_ref, *refs):
    pieces, refs = (refs[:10], refs[10:]) if blocked else (refs[:2], refs[2:])
    out_ref, g_resid1_ref, g_attn_ref, g_vec_ref = refs[:4]
    count = 4 if blocked else 2
    outs, refs = refs[4 : 4 + count], refs[4 + count :]
    made, refs = refs[:count], refs[count:]
    up, down, act, slope, low, acc, sems = refs
    rows, width = resid1_ref.shape
    blocks = up.shape[0]
    me = me_ref[0]
    share = width // devices
    long = share * blocks

    if blocked:
        for array, far, relative, top, bottom in piece_blocks(devices, 2 * long, long):
            piece = pieces[array].at[far]
            if bottom > long:
                row = pl.multiple_of((relative ^ me) * share, 8)
                for b in range(blocks):
                    pltpu.make_async_copy(
                        piece.at[pl.ds(long + b * share - top, share)],
                        up.at[b, pl.ds(row, share)],
                        sems.at[0],
                    ).start()
            if top == 0:
                row = pl.multiple_of((relative ^ me) * long, 8)
                pltpu.make_async_copy(
                    piece.at[pl.ds(0, long)], down.at[pl.ds(row, long)], sems.at[1]
                ).start()
    else:
        pltpu.make_async_copy(pieces[0], down, sems.at[1]).start()
        pltpu.make_async_copy(pieces[1], up, sems.at[0]).start()

    gain_one, shift_one, bdown, gain_two, shift_two = (vec_ref[i : i + 1, :] for i in range(3, 8))
    hidden1, normed1, inverse1 = layer_norm(resid1_ref[...], gain_one, shift_one)
    low[...] = hidden1.astype(BF16)
    acc[...] = hidden1 + bdown
    all_done(up, sems.at[0])
    all_done(down, sems.at[1])

    def forward(b, carry):
        pre = dot_nn(low[...], up[b]) + vec_ref[pl.ds(8 + b, 1), :]
        cdf = 0.5 * (1.0 + lax.erf(pre * ROOT_HALF))
        slope[b] = cdf + pre * (jnp.exp(-0.5 * pre * pre) * INV_ROOT_TAU)
        activated = (pre * cdf).astype(BF16)
        act[b] = activated
        acc[...] += dot_nn(activated, down[pl.ds(pl.multiple_of(b * width, width), width)])
        return carry

    lax.fori_loop(0, blocks, forward, 0)

    g_vec_ref[...] = jnp.zeros_like(g_vec_ref)
    result, normed2, inverse2 = layer_norm(acc[...], gain_two, shift_two)
    valid = lax.broadcasted_iota(jnp.int32, (rows, 1), 0) < count_ref[0]
    out_ref[...] = jnp.where(valid, result, 0.0).astype(BF16)
    g_out = jnp.where(valid, cot_ref[...].astype(F32), 0.0)
    g_vec_ref[6:7, :] = jnp.sum(g_out * normed2, axis=0, keepdims=True)
    g_vec_ref[7:8, :] = jnp.sum(g_out, axis=0, keepdims=True)
    g_resid2 = norm_back(g_out, normed2, inverse2, gain_two)
    acc[...] = g_resid2
    g_ffn = g_resid2.astype(BF16)
    g_vec_ref[5:6, :] = jnp.sum(g_ffn.astype(F32), axis=0, keepdims=True)

    def backward(b, carry):
        start = pl.multiple_of(b * width, width)
        down_b = down[pl.ds(start, width)]
        g_down = dot_tn(act[b], g_ffn).astype(BF16)
        if blocked:
            per = width // long // 2
            for i in range(per):
                pair = (g_down[(2 * i + j) * long : (2 * i + j + 1) * long] for j in range(2))
                index = (b * per + i) ^ (me >> 1)
                paired_store(pair, index, me & 1, *made[:2])
                for k in range(2):
                    pltpu.make_async_copy(
                        made[k].at[index], outs[k].at[index], sems.at[2 + k]
                    ).start()
        else:
            made[0][pl.ds(start, width)] = g_down
        g_pre = (dot_nt(g_ffn, down_b) * slope[b]).astype(BF16)
        g_vec_ref[pl.ds(8 + b, 1), :] = jnp.sum(g_pre.astype(F32), axis=0, keepdims=True)
        g_up = dot_tn(low[...], g_pre).astype(BF16)
        if blocked:
            for i in range(devices // 2):
                pair = (g_up[(2 * i + j) * share : (2 * i + j + 1) * share] for j in range(2))
                index = i ^ (me >> 1)
                paired_store(pair, (index, b), me & 1, *made[2:])
                for k in range(2, 4):
                    pltpu.make_async_copy(
                        made[k].at[index, b], outs[k].at[index, b], sems.at[2 + k]
                    ).start()
        else:
            made[1][b] = g_up
        acc[...] += dot_nt(g_pre, up[b])
        return carry

    lax.fori_loop(0, blocks, backward, 0)
    if not blocked:
        for k in range(2):
            pltpu.make_async_copy(made[k], outs[k], sems.at[2 + k]).start()
    g_hidden1 = acc[...]
    g_vec_ref[3:4, :] = jnp.sum(g_hidden1 * normed1, axis=0, keepdims=True)
    g_vec_ref[4:5, :] = jnp.sum(g_hidden1, axis=0, keepdims=True)
    g_resid1 = norm_back(g_hidden1, normed1, inverse1, gain_one)
    g_resid1_ref[...] = g_resid1
    g_attn = g_resid1.astype(BF16)
    g_attn_ref[...] = g_attn
    g_vec_ref[2:3, :] = jnp.sum(g_attn.astype(F32), axis=0, keepdims=True)
    for k in range(count):
        all_done(made[k], sems.at[2 + k])


def feed_forward(me, devices, hidden, count, resid1, cotangent, vectors, pieces):
    rows, width = resid1.shape
    share = width // devices
    blocks = hidden // width
    long = hidden // devices
    blocked = share % 8 == 0
    if blocked:
        g_shapes = [(devices // 2, long, width)] * 2 + [(devices // 2, blocks, share, width)] * 2
    else:
        rows_of = natural(pieces)
        up = rows_of[:, long:].reshape(devices, blocks, share, width).transpose(1, 0, 2, 3)
        pieces = (rows_of[:, :long].reshape(hidden, width), up.reshape(blocks, width, width))
        g_shapes = [(hidden, width), (blocks, width, width)]
    vmem = pl.BlockSpec(memory_space=pltpu.VMEM)
    smem = pl.BlockSpec(memory_space=pltpu.SMEM)
    any_space = pl.BlockSpec(memory_space=pl.ANY)
    outs = pl.pallas_call(
        partial(feed_forward_kernel, blocked, devices),
        in_specs=[smem, smem] + [vmem] * 3 + [any_space] * len(pieces),
        out_specs=[vmem] * 4 + [any_space] * len(g_shapes),
        out_shape=[
            jax.ShapeDtypeStruct((rows, width), BF16),
            jax.ShapeDtypeStruct((rows, width), F32),
            jax.ShapeDtypeStruct((rows, width), BF16),
            jax.ShapeDtypeStruct((16, width), F32),
        ]
        + [jax.ShapeDtypeStruct(shape, BF16) for shape in g_shapes],
        scratch_shapes=[pltpu.VMEM(shape, BF16) for shape in g_shapes]
        + [
            pltpu.VMEM((blocks, width, width), BF16),
            pltpu.VMEM((hidden, width), BF16),
            pltpu.VMEM((blocks, rows, width), BF16),
            pltpu.VMEM((blocks, rows, width), F32),
            pltpu.VMEM((rows, width), BF16),
            pltpu.VMEM((rows, width), F32),
            pltpu.SemaphoreType.DMA((6,)),
        ],
        compiler_params=pltpu.CompilerParams(vmem_limit_bytes=60 << 20),
        cost_estimate=pl.CostEstimate(
            flops=12 * rows * width * hidden,
            transcendentals=2 * rows * hidden,
            bytes_accessed=8 * width * hidden + 16 * rows * width,
        ),
    )(me, count, resid1, cotangent, vectors, *pieces)
    if blocked:
        return outs
    g_down = in_order(outs[4].reshape(devices, long, width))
    g_up = in_order(outs[5].reshape(blocks, devices, share, width).transpose(1, 0, 2, 3))
    pairs = [g.reshape((devices // 2, 2) + g.shape[1:]) for g in (g_down, g_up)]
    return list(outs[:4]) + [g[:, i] for g in pairs for i in range(2)]


def flip(array, stride):
    devices = lax.axis_size("dev")
    return lax.ppermute(array, "dev", [(i, i ^ stride) for i in range(devices)])


def gather_far(shard):
    blocks = [shard]
    for k in range(1, lax.axis_size("dev") // 8):
        low = k & -k
        blocks.append(flip(blocks[k - low], 8 * low))
    return blocks


def plane_neighbours(line):
    return flip(line, 2), flip(line, 4)


def plane_corner(across_x, across_y):
    return flip(across_x, 4), flip(across_y, 2)


def in_order(blocks):
    devices = blocks.shape[0]
    order = jnp.arange(devices, dtype=jnp.int32) ^ lax.axis_index("dev")
    return jnp.take(blocks, order, axis=0, mode="clip")


def add_low(left, right):
    return (left.astype(F32) + right.astype(F32)).astype(BF16)


def near_shape(block):
    return block.reshape((block.shape[0] // 4, 2, 2) + block.shape[1:])


def take(array, axis, index):
    return lax.index_in_dim(array, index, axis, keepdims=False)


def stage_sums(kept, got, axis):
    return tuple(add_low(take(kept, axis, i), take(got, axis, i)) for i in range(2))


def far_halves(part):
    pairs = part.reshape((part.shape[0] // 2, 2) + part.shape[1:])
    return pairs[:, 0], pairs[:, 1]


def scatter_far(part, stride, rows):
    while part.shape[0] > 1:
        keep, send = far_halves(part)
        got = flip(send, stride)
        if rows is not None:
            got, other = tied(got, flip(rows, stride))
            rows = rows + other
        part = add_low(keep, got) if part.shape[0] > 2 else keep.astype(F32) + got
        stride *= 2
    return part[0].astype(F32), rows


def tied(*values):
    return lax.optimization_barrier(values)


def shards(
    tokens,
    cotangent,
    lengths,
    dealing,
    w_query,
    w_key,
    w_value,
    w_out,
    b_query,
    b_value,
    b_out,
    norm1_gain,
    norm1_bias,
    w_up,
    b_up,
    w_down,
    b_down,
    norm2_gain,
    norm2_bias,
):
    devices = lax.axis_size("dev")
    me = lax.axis_index("dev")
    seq_count, local_len, width = tokens.shape
    per_device = seq_count // devices
    longest = local_len * devices
    capacity = cotangent.shape[0]
    share = w_query.shape[0]
    hidden = w_up.shape[1]

    outgoing = jnp.take(tokens, dealing, axis=0, mode="clip").reshape(devices, per_device, local_len, width)

    vectors = (
        b_query,
        b_value,
        b_out,
        norm1_gain,
        norm1_bias,
        b_down,
        norm2_gain,
        norm2_bias,
    )
    own_attn, own_ffn = prepare(
        me.reshape(1), (w_query, w_key, w_value, w_out), w_up, w_down, vectors, b_up
    )
    long = hidden // devices
    attn_line, ffn_line = gather_far(own_attn), gather_far(own_ffn)
    attn_line = jnp.stack(attn_line)
    attn_x, attn_y = plane_neighbours(attn_line)
    corner = attn_x[:, : 2 * share], attn_y[:, 2 * share :]
    outgoing, _, _, *ffn_line = tied(outgoing, *corner, *ffn_line)
    arrived = lax.all_to_all(outgoing, "dev", 0, 0)
    attn_own = (attn_line, attn_x, attn_y, *plane_corner(*corner))
    attn_pieces = (*attn_own, *(flip(block, 1) for block in attn_own))
    ffn_line = jnp.stack(ffn_line)
    ffn_x, ffn_y = plane_neighbours(ffn_line)

    my_slots = lax.dynamic_slice_in_dim(dealing, me * per_device, per_device)
    slot_len = jnp.take(lengths, my_slots)
    slot_ends = jnp.cumsum(slot_len)
    starts = slot_ends - slot_len
    row_ids = jnp.arange(capacity, dtype=jnp.int32)
    segment = jnp.sum((row_ids[:, None] >= slot_ends[None, :]).astype(jnp.int32), axis=1)
    is_valid = segment < per_device
    bounds = jnp.concatenate([starts, slot_ends[-1:]])
    picked = segment[:, None] == jnp.arange(per_device + 1, dtype=jnp.int32)[None, :]
    position = row_ids - jnp.sum(jnp.where(picked, bounds[None, :], 0), axis=1)
    source = (position // local_len) * (per_device * local_len) + segment * local_len
    source = jnp.where(is_valid, source + position % local_len, -1)

    packed, queries, key_rows, value_rows, context, log_total, resid1, vector_rows, weights = (
        attention_forward(
            me.reshape(1),
            devices,
            segment,
            source,
            arrived.reshape(-1, width),
            attn_pieces,
        )
    )

    ffn_x, ffn_y, resid1 = tied(ffn_x, ffn_y, resid1)
    ffn_own = (ffn_line, ffn_x, ffn_y, *plane_corner(ffn_x[:, :long], ffn_y[:, long:]))
    ffn_pieces = (*ffn_own, *(flip(block, 1) for block in ffn_own))
    layer_out, g_resid1, g_attn, g_rows, a_keep, a_send, b_keep, b_send = feed_forward(
        me.reshape(1), devices, hidden, slot_ends[-1:], resid1, cotangent, vector_rows, ffn_pieces
    )

    col_blocks = hidden // width
    own_far = devices // 8

    got_a, got_b = flip(a_send, 1), flip(b_send, 1)
    backward = partial(attention_backward, segment=segment, log_total=log_total, weights=weights)
    operands = dict(queries=queries, key_rows=key_rows, value_rows=value_rows)
    grads_0 = backward(0, 1, g_attn=g_attn, **operands)
    got_a, got_b, *grads_0 = tied(got_a, got_b, *grads_0)
    a_keep, a_send = stage_sums(near_shape(a_keep), near_shape(got_a), 2)
    b_keep, b_send = stage_sums(near_shape(b_keep), near_shape(got_b), 1)
    a_send, b_send, g_attn_late = tied(a_send, b_send, g_attn)
    got_a, got_b = flip(a_send, 2), flip(b_send, 4)
    grads_1 = backward(1, width // GROUP, g_attn=g_attn_late, **operands)
    step_ids = jnp.arange(longest, dtype=jnp.int32).reshape(devices, 1, local_len)
    inside = step_ids < slot_len[None, :, None]
    take_rows = jnp.where(inside, starts[None, :, None] + step_ids, -1).reshape(-1)
    gradients = (grads_0, grads_1)
    unpacked = input_gradient(take_rows, g_resid1, weights, gradients)
    got_a, got_b, unpacked, g_attn_late, *grads_1 = tied(
        got_a, got_b, unpacked, g_attn_late, *grads_1
    )
    returned = lax.all_to_all(
        unpacked.reshape(devices, per_device, local_len, width), "dev", 0, 0
    )
    a_keep, a_send = stage_sums(a_keep, got_a, 1)
    b_keep, b_send = stage_sums(b_keep, got_b, 1)
    got_a, got_b = flip(a_send, 4), flip(b_send, 2)

    c_keep, c_send, d_keep, d_send, g_rows_attn = weight_gradients(
        me.reshape(1), devices, packed, context, g_attn_late, (grads_0, grads_1)
    )
    g_rows = g_rows + jnp.pad(g_rows_attn, ((0, 8), (0, 0)))
    got_a, got_b, got_c, got_d, g_other = tied(
        got_a, got_b, flip(c_send, 1), flip(d_send, 1), flip(g_rows, 1)
    )
    ffn_part = jnp.concatenate(
        [
            add_low(a_keep, got_a),
            add_low(b_keep, got_b).reshape(own_far, -1, width),
        ],
        axis=1,
    )
    ffn_keep, ffn_send = far_halves(ffn_part)
    ffn_got = flip(ffn_send, 8)
    c_keep, c_send = stage_sums(near_shape(c_keep), near_shape(got_c), 2)
    d_keep, d_send = stage_sums(near_shape(d_keep), near_shape(got_d), 1)
    g_rows = g_rows + g_other
    got_c, got_d, g_other = tied(flip(c_send, 2), flip(d_send, 4), flip(g_rows, 2))
    c_keep, c_send = stage_sums(c_keep, got_c, 1)
    d_keep, d_send = stage_sums(d_keep, got_d, 1)
    g_rows = g_rows + g_other
    ffn_got, got_c, got_d, g_other, returned = tied(
        ffn_got, flip(c_send, 4), flip(d_send, 2), flip(g_rows, 4), returned
    )
    ffn_part = add_low(ffn_keep, ffn_got)
    attn_part = jnp.concatenate([add_low(c_keep, got_c), add_low(d_keep, got_d)], axis=1)
    g_rows = g_rows + g_other
    attn_keep, attn_send = far_halves(attn_part)
    attn_got, g_other = tied(flip(attn_send, 8), flip(g_rows, 8))
    attn_part = add_low(attn_keep, attn_got)
    g_rows = g_rows + g_other
    ffn_sum, _ = scatter_far(ffn_part, 16, None)
    attn_sum, g_rows = scatter_far(attn_part, 16, g_rows)
    g_wdown = ffn_sum[:long]
    g_wup = ffn_sum[long:].reshape(col_blocks, share, width)
    g_wup = g_wup.transpose(1, 0, 2).reshape(share, hidden)
    own_vec = lax.dynamic_slice_in_dim(g_rows[:8], me * share, share, axis=1)
    up_rows = g_rows[8 : 8 + col_blocks].reshape(hidden)
    own_up = lax.dynamic_slice_in_dim(up_rows, me * (hidden // devices), hidden // devices)

    slots = jnp.arange(seq_count, dtype=jnp.int32)
    inverse_deal = jnp.sum(jnp.where(dealing[None, :] == slots[:, None], slots[None, :], 0), axis=1)
    returned = returned.reshape(seq_count, local_len, width)
    input_grad = jnp.take(returned, inverse_deal, axis=0, mode="clip")
    return (
        layer_out,
        input_grad,
        attn_sum[0],
        attn_sum[1],
        attn_sum[2],
        attn_sum[3],
        own_vec[0],
        own_vec[1],
        own_vec[2],
        own_vec[3],
        own_vec[4],
        g_wup,
        own_up,
        g_wdown,
        own_vec[5],
        own_vec[6],
        own_vec[7],
    )


def solution(mesh):
    rows = P("dev", None)
    vector = P("dev")
    seqs = P(None, "dev", None)
    return jax.shard_map(
        shards,
        mesh=mesh,
        in_specs=(
            (seqs, rows, P(), P())
            + (rows,) * 4
            + (vector,) * 5
            + (rows, vector, rows)
            + (vector,) * 3
        ),
        out_specs=(
            (rows, seqs) + (rows,) * 4 + (vector,) * 5 + (rows, vector, rows) + (vector,) * 3
        ),
        check_vma=False,
    )
```

```python
from functools import partial

import jax
import jax.numpy as jnp
from jax import lax
from jax.experimental import pallas as pl
from jax.experimental.pallas import tpu as pltpu
from jax.sharding import PartitionSpec as P

HEADS = 12
HEAD_DIM = 64
PAIR = 2 * HEAD_DIM
GROUP = 4 * HEAD_DIM

MASKED_SCORE = -1e30
ROOT_HALF = 0.7071067811865476
INV_ROOT_TAU = 0.3989422804014327
BF16 = jnp.bfloat16
F32 = jnp.float32


def layer_norm(residual, norm_gain, norm_shift):
    center = residual - jnp.mean(residual, axis=-1, keepdims=True)
    inverse = lax.rsqrt(jnp.mean(center * center, axis=-1, keepdims=True) + 1e-05)
    normed = center * inverse
    return (normed * norm_gain + norm_shift, normed, inverse)


def norm_back(upstream, normed, inverse, norm_gain):
    scaled = upstream * norm_gain
    return inverse * (
        scaled
        - jnp.mean(scaled, axis=-1, keepdims=True)
        - normed * jnp.mean(scaled * normed, axis=-1, keepdims=True)
    )


def dot_nt(left, right):
    return lax.dot_general(left, right, (((1,), (1,)), ((), ())), preferred_element_type=F32)


def dot_nn(left, right):
    return lax.dot_general(left, right, (((1,), (0,)), ((), ())), preferred_element_type=F32)


def piece_blocks(devices, height, split):
    for core in range(2):
        for far in range(devices // 8):
            for near in range(4):
                relative = core + 2 * near + 8 * far
                if near < 3:
                    yield 5 * core + near, far, relative, 0, height
                else:
                    yield 5 * core + 3, far, relative, 0, split
                    yield 5 * core + 4, far, relative, split, height


def all_done(ref, sem):
    pltpu.make_async_copy(ref, ref, sem).wait()


def prepare_kernel(me_ref, *refs):
    weights, up_ref, down_ref, vectors, b_up = refs[:4], refs[4], refs[5], refs[6:14], refs[14]
    attn_ref, ffn_ref, rows_ref = refs[15:]
    share, width = weights[0].shape
    long = b_up.shape[1]
    me = me_ref[0]
    for i, weight in enumerate(weights):
        attn_ref[i * share : (i + 1) * share] = weight[...]
    ffn_ref[:long] = down_ref[...]
    for b in range(long // share):
        row = long + b * share
        ffn_ref[row : row + share] = up_ref[:, b * width : (b + 1) * width]
    rows_ref[...] = jnp.zeros_like(rows_ref)
    for i, vector in enumerate(vectors):
        rows_ref[i : i + 1, 0:share] = vector[...].astype(F32)
    for i in range(8, 16):
        rows_ref[i : i + 1, 0:long] = b_up[...].astype(F32)
    values = rows_ref[...].astype(BF16)
    shape = (values.shape[1], width)
    source = lax.broadcasted_iota(jnp.int32, shape, 0)
    target = lax.broadcasted_iota(jnp.int32, shape, 1)
    moved = []
    for start in (me * share, (me * long) % width):
        here = jnp.where(target == source + start, 1.0, 0.0).astype(BF16)
        moved.append(dot_nn(values, here))
    row = lax.broadcasted_iota(jnp.int32, moved[0].shape, 0)
    of_up = jnp.where(row == 8 + (me * long) // width, moved[1], 0.0)
    attn_ref[4 * share :] = jnp.where(row < 8, moved[0], of_up).astype(BF16)


def prepare(me, weights, w_up, w_down, vectors, b_up):
    share, width = weights[0].shape
    long = w_down.shape[0]
    vmem = pl.BlockSpec(memory_space=pltpu.VMEM)
    smem = pl.BlockSpec(memory_space=pltpu.SMEM)
    rows = [vector.reshape(1, -1) for vector in vectors + (b_up,)]
    return pl.pallas_call(
        prepare_kernel,
        in_specs=[smem] + [vmem] * 15,
        out_specs=[vmem] * 2,
        out_shape=[
            jax.ShapeDtypeStruct((4 * share + 16, width), BF16),
            jax.ShapeDtypeStruct((2 * long, width), BF16),
        ],
        scratch_shapes=[pltpu.VMEM((16, PAIR), F32)],
        cost_estimate=pl.CostEstimate(flops=1 << 22, transcendentals=0, bytes_accessed=1 << 20),
    )(me, *weights, w_up, w_down, *rows)


def projection_kernel(blocked, devices, me_ref, source_ref, arrived_ref, *refs):
    pieces, refs = (refs[:10], refs[10:]) if blocked else (refs[:2], refs[2:])
    packed_ref, q_ref, k_ref, v_ref, vec_ref, w_out_ref, weights, vec_rows, sems = refs
    rows, width = packed_ref.shape
    share = width // devices
    me = me_ref[0]
    if blocked:
        height = 4 * share + 16
        for array, far, relative, top, bottom in piece_blocks(devices, height, 2 * share):
            row = pl.multiple_of((relative ^ me) * share, 8)
            for i in range(top // share, min(bottom // share, 4)):
                pltpu.make_async_copy(
                    pieces[array].at[far, pl.ds(i * share - top, share)],
                    weights.at[i, pl.ds(row, share)],
                    sems.at[0],
                ).start()
            if bottom == height:
                pltpu.make_async_copy(
                    pieces[array].at[far, pl.ds(4 * share - top, 16)],
                    vec_rows.at[relative],
                    sems.at[1],
                ).start()
    else:
        pltpu.make_async_copy(pieces[0], weights, sems.at[0]).start()
        pltpu.make_async_copy(pieces[1], vec_rows, sems.at[1]).start()
    places = arrived_ref.shape[0]
    block = rows // 4
    for i in range(4):
        here = slice(i * block, (i + 1) * block)
        pick = source_ref[here] == lax.broadcasted_iota(jnp.int32, (block, places), 1)
        pick = jnp.where(pick, 1.0, 0.0).astype(BF16)
        packed_ref[here] = dot_nn(pick, arrived_ref[...]).astype(BF16)
    all_done(vec_rows, sems.at[1])
    vec_ref[...] = jnp.sum(vec_rows[...].astype(F32), axis=0)
    all_done(weights, sems.at[0])
    out_copy = pltpu.make_async_copy(weights, w_out_ref, sems.at[2])
    out_copy.start()
    packed = packed_ref[...]
    q_ref[...] = ((dot_nn(packed, weights[0]) + vec_ref[0:1, :]) * 0.125).astype(BF16)
    k_ref[...] = dot_nn(packed, weights[1]).astype(BF16)
    v_ref[...] = (dot_nn(packed, weights[2]) + vec_ref[1:2, :]).astype(BF16)
    out_copy.wait()


def attention_forward_kernel(
    seg_col, seg_row, packed_ref, vec_ref, q_ref, k_ref, v_ref, wo_ref, ctx_ref, lse_ref, resid_ref, bias
):
    step = pl.program_id(0)
    rows = q_ref.shape[0]

    @pl.when(step == 0)
    def _():
        bias[...] = jnp.where(seg_col[...] == seg_row[...], 0.0, MASKED_SCORE)
        resid_ref[...] = packed_ref[...].astype(F32) + vec_ref[2:3, :]

    lane = lax.broadcasted_iota(jnp.int32, (rows, PAIR), 1)
    stats = lse_ref[...]
    for pair in range(GROUP // PAIR):
        span = slice(pair * PAIR, (pair + 1) * PAIR)
        q_pair, k_pair, v_pair = q_ref[:, span], k_ref[:, span], v_ref[:, span]
        outs = []
        for half in range(2):
            own = (lane // HEAD_DIM) == half
            q_own = jnp.where(own, q_pair, jnp.zeros_like(q_pair))
            scores = dot_nt(q_own, k_pair) + bias[...]
            top = jnp.max(scores, axis=1, keepdims=True)
            exped = jnp.exp(scores - top)
            total = jnp.sum(exped, axis=1, keepdims=True)
            outs.append(dot_nn(exped.astype(BF16), v_pair) * (1.0 / total))
            head = step * (GROUP // HEAD_DIM) + pair * 2 + half
            stats = jnp.where(lane == head, top + jnp.log(total), stats)
        ctx_ref[:, span] = jnp.where(lane < HEAD_DIM, outs[0], outs[1]).astype(BF16)
    lse_ref[...] = stats
    resid_ref[...] += dot_nn(ctx_ref[...], wo_ref[...])


def natural(pieces):
    corners = [jnp.concatenate(pieces[i + 3 : i + 5], axis=1) for i in (0, 5)]
    blocks = jnp.stack(
        [b for i, corner in zip((0, 5), corners) for b in (*pieces[i : i + 3], corner)], axis=1
    )
    far = blocks.shape[0]
    blocks = blocks.reshape((far, 2, 4) + blocks.shape[2:]).swapaxes(1, 2)
    return in_order(blocks.reshape((8 * far,) + blocks.shape[3:]))


def projections(me, devices, source, arrived, pieces):
    rows, width = source.shape[0], arrived.shape[1]
    share = width // devices
    blocked = share % 8 == 0
    if not blocked:
        rows_of = natural(pieces)
        parts = [rows_of[:, i * share : (i + 1) * share].reshape(width, width) for i in range(4)]
        pieces = (jnp.stack(parts), rows_of[:, 4 * share :])
    vmem = pl.BlockSpec(memory_space=pltpu.VMEM)
    any_space = pl.BlockSpec(memory_space=pl.ANY)
    return pl.pallas_call(
        partial(projection_kernel, blocked, devices),
        in_specs=[pl.BlockSpec(memory_space=pltpu.SMEM), vmem, vmem] + [any_space] * len(pieces),
        out_specs=[vmem] * 5 + [any_space],
        out_shape=[jax.ShapeDtypeStruct((rows, width), BF16)] * 4
        + [
            jax.ShapeDtypeStruct((16, width), F32),
            jax.ShapeDtypeStruct((4, width, width), BF16),
        ],
        scratch_shapes=[
            pltpu.VMEM((4, width, width), BF16),
            pltpu.VMEM((devices, 16, width), BF16),
            pltpu.SemaphoreType.DMA((3,)),
        ],
        compiler_params=pltpu.CompilerParams(vmem_limit_bytes=40 << 20),
        cost_estimate=pl.CostEstimate(
            flops=6 * rows * width * width + 2 * rows * width * arrived.shape[0],
            transcendentals=0,
            bytes_accessed=16 * width * width + rows * width * 10,
        ),
    )(me, source[:, None], arrived, *pieces)


def attention_forward(segment, packed, vectors, queries, key_rows, value_rows, weights):
    rows, width = packed.shape
    block = pl.BlockSpec((rows, GROUP), lambda g: (0, g))
    whole = lambda shape: pl.BlockSpec(shape, lambda g: (0, 0))
    return pl.pallas_call(
        attention_forward_kernel,
        grid=(width // GROUP,),
        in_specs=[
            whole((rows, 1)),
            whole((1, rows)),
            whole((rows, width)),
            whole((16, width)),
            block,
            block,
            block,
            pl.BlockSpec((None, GROUP, width), lambda g: (3, g, 0)),
        ],
        out_specs=[block, whole((rows, PAIR)), whole((rows, width))],
        out_shape=[
            jax.ShapeDtypeStruct((rows, width), BF16),
            jax.ShapeDtypeStruct((rows, PAIR), F32),
            jax.ShapeDtypeStruct((rows, width), F32),
        ],
        scratch_shapes=[pltpu.VMEM((rows, rows), F32)],
        compiler_params=pltpu.CompilerParams(vmem_limit_bytes=48 << 20),
        cost_estimate=pl.CostEstimate(
            flops=HEADS * rows * rows * PAIR * 4 + 2 * rows * width * width,
            transcendentals=HEADS * rows * rows,
            bytes_accessed=2 * width * width + rows * width * 14,
        ),
    )(
        segment[:, None],
        segment[None, :],
        packed,
        vectors,
        queries,
        key_rows,
        value_rows,
        weights,
    )


def attention_backward_kernel(
    first,
    seg_col,
    seg_row,
    lse_ref,
    g_attn_ref,
    w_out_ref,
    q_ref,
    k_ref,
    v_ref,
    dq_ref,
    dk_ref,
    dv_ref,
    bias,
):
    step = pl.program_id(0)

    @pl.when(step == 0)
    def _():
        bias[...] = jnp.where(seg_col[...] == seg_row[...], 0.0, MASKED_SCORE)

    rows = q_ref.shape[0]
    lane = lax.broadcasted_iota(jnp.int32, (rows, PAIR), 1)
    g_context = dot_nt(g_attn_ref[...], w_out_ref[...]).astype(BF16)
    for pair in range(GROUP // PAIR):
        span = slice(pair * PAIR, (pair + 1) * PAIR)
        q_pair, k_pair, v_pair = q_ref[:, span], k_ref[:, span], v_ref[:, span]
        g_pair = g_context[:, span]
        q_turn, g_turn = q_pair.T, g_pair.T
        dq, dk, dv = [], [], []
        for half in range(2):
            own = (lane // HEAD_DIM) == half
            part = slice(half * HEAD_DIM, (half + 1) * HEAD_DIM)
            zero = jnp.zeros_like(q_pair)
            head = (first + step) * (GROUP // HEAD_DIM) + pair * 2 + half
            log_total = jnp.sum(jnp.where(lane == head, lse_ref[...], 0.0), axis=1, keepdims=True)
            scores = dot_nt(jnp.where(own, q_pair, zero), k_pair) + bias[...]
            probs = jnp.exp(scores - log_total)
            low = probs.astype(BF16)
            g_probs = dot_nt(jnp.where(own, g_pair, zero), v_pair)
            product = probs * g_probs
            g_scores = (product - probs * jnp.sum(product, axis=1, keepdims=True)).astype(BF16)
            dq.append(dot_nn(g_scores, k_pair))
            dk.append(dot_nn(q_turn[part], g_scores))
            dv.append(dot_nn(g_turn[part], low))
        dq_ref[:, span] = jnp.where(lane < HEAD_DIM, dq[0], dq[1]).astype(BF16)
        dk_ref[:, span] = jnp.concatenate(dk, axis=0).T.astype(BF16)
        dv_ref[:, span] = jnp.concatenate(dv, axis=0).T.astype(BF16)


def attention_backward(first, last, segment, log_total, g_attn, weights, queries, key_rows, value_rows):
    rows, width = queries.shape
    taken = pl.BlockSpec((rows, GROUP), lambda g: (0, g + first))
    made = pl.BlockSpec((rows, GROUP), lambda g: (0, g))
    whole = lambda shape: pl.BlockSpec(shape, lambda g: (0, 0))
    count = last - first
    return pl.pallas_call(
        partial(attention_backward_kernel, first),
        grid=(count,),
        in_specs=[
            whole((rows, 1)),
            whole((1, rows)),
            whole((rows, PAIR)),
            whole((rows, width)),
            pl.BlockSpec((None, GROUP, width), lambda g: (3, g + first, 0)),
        ]
        + [taken] * 3,
        out_specs=[made] * 3,
        out_shape=[jax.ShapeDtypeStruct((rows, count * GROUP), BF16)] * 3,
        scratch_shapes=[pltpu.VMEM((rows, rows), F32)],
        compiler_params=pltpu.CompilerParams(vmem_limit_bytes=48 << 20),
        cost_estimate=pl.CostEstimate(
            flops=count * 4 * rows * rows * PAIR * 10,
            transcendentals=count * 4 * rows * rows,
            bytes_accessed=count * rows * GROUP * 14,
        ),
    )(segment[:, None], segment[None, :], log_total, g_attn, weights, queries, key_rows, value_rows)


def input_gradient_kernel(parts, row_ref, resid_ref, w_ref, *refs):
    out_ref = refs[-1]
    rows = resid_ref.shape[0]
    total = resid_ref[...]
    column = 0
    for i in range(parts):
        dq, dk, dv = (refs[3 * i + j] for j in range(3))
        span = slice(column, column + dq.shape[1])
        column += dq.shape[1]
        total += dot_nt(dq[...], w_ref[0, :, span]) * 0.125
        total += dot_nt(dk[...], w_ref[1, :, span])
        total += dot_nt(dv[...], w_ref[2, :, span])
    g_input = total.astype(BF16)
    places = row_ref.shape[0]
    block = places // 4
    for i in range(4):
        here = slice(i * block, (i + 1) * block)
        pick = row_ref[here] == lax.broadcasted_iota(jnp.int32, (block, rows), 1)
        pick = jnp.where(pick, 1.0, 0.0).astype(BF16)
        out_ref[here] = dot_nn(pick, g_input).astype(BF16)


def input_gradient(take_rows, g_resid1, weights, gradients):
    rows, width = g_resid1.shape
    places = take_rows.shape[0]
    flat = [g for group in gradients for g in group]
    vmem = pl.BlockSpec(memory_space=pltpu.VMEM)
    return pl.pallas_call(
        partial(input_gradient_kernel, len(gradients)),
        in_specs=[vmem] * (3 + len(flat)),
        out_specs=vmem,
        out_shape=jax.ShapeDtypeStruct((places, width), BF16),
        compiler_params=pltpu.CompilerParams(vmem_limit_bytes=48 << 20),
        cost_estimate=pl.CostEstimate(
            flops=6 * rows * width * width + 2 * places * rows * width,
            transcendentals=0,
            bytes_accessed=12 * width * width + 10 * rows * width + 2 * places * width,
        ),
    )(take_rows[:, None], g_resid1, weights, *flat)


def paired_store(values, index, core, keep_ref, send_ref):
    low, high = values
    first = core == 0
    keep_ref[index] = jnp.where(first, low, high)
    send_ref[index] = jnp.where(first, high, low)


def weight_gradient_kernel(blocked, parts, me_ref, x_ref, ctx_ref, g_attn_ref, *refs):
    ins, outs = refs[: 3 * parts], refs[3 * parts :]
    rows, width = x_ref.shape
    me = me_ref[0]
    core = me & 1
    vec_ref = outs[-1]
    vec_ref[...] = jnp.zeros_like(vec_ref)

    def store(kind, grad):
        if not blocked:
            outs[0][kind] = grad
            return
        keep, send = (outs[2 * (kind // 2) + i] for i in range(2))
        share = keep.shape[2]
        for i in range(keep.shape[0]):
            low, high = (grad[(2 * i + j) * share : (2 * i + j + 1) * share] for j in range(2))
            paired_store((low, high), (i ^ (me >> 1), kind % 2), core, keep, send)

    x_turn = x_ref[...].T
    for j in range(3):
        pieces = []
        for i in range(parts):
            grads = ins[3 * i + j][...]
            span = slice(i * grads.shape[1], (i + 1) * grads.shape[1])
            piece = dot_nn(x_turn, grads)
            pieces.append((piece * 0.125 if j == 0 else piece).astype(BF16))
        store(j, jnp.concatenate(pieces, axis=1))
    store(3, dot_tn(ctx_ref[...], g_attn_ref[...]).astype(BF16))
    column = 0
    for i in range(parts):
        dq, _, dv = (ins[3 * i + j][...].astype(F32) for j in range(3))
        span = slice(column, column + dq.shape[1])
        column += dq.shape[1]
        vec_ref[0:1, span] = jnp.sum(dq, axis=0, keepdims=True) * 0.125
        vec_ref[1:2, span] = jnp.sum(dv, axis=0, keepdims=True)


def weight_gradients(me, devices, packed, context, g_attn, gradients):
    rows, width = packed.shape
    share = width // devices
    blocked = share % 8 == 0
    flat = [g for group in gradients for g in group]
    vmem = pl.BlockSpec(memory_space=pltpu.VMEM)
    smem = pl.BlockSpec(memory_space=pltpu.SMEM)
    if blocked:
        shapes = [jax.ShapeDtypeStruct((devices // 2, 2, share, width), BF16)] * 4
    else:
        shapes = [jax.ShapeDtypeStruct((4, width, width), BF16)]
    shapes.append(jax.ShapeDtypeStruct((8, width), F32))
    outs = pl.pallas_call(
        partial(weight_gradient_kernel, blocked, len(gradients)),
        in_specs=[smem] + [vmem] * (3 + len(flat)),
        out_specs=[vmem] * len(shapes),
        out_shape=shapes,
        compiler_params=pltpu.CompilerParams(vmem_limit_bytes=48 << 20),
        cost_estimate=pl.CostEstimate(
            flops=8 * rows * width * width,
            transcendentals=0,
            bytes_accessed=8 * width * width + 12 * rows * width,
        ),
    )(me, packed, context, g_attn, *flat)
    if blocked:
        return outs
    grads = in_order(outs[0].reshape(4, devices, share, width).transpose(1, 0, 2, 3))
    grads = grads.reshape(devices // 2, 2, 4, share, width)
    return [grads[:, i, j : j + 2] for j in (0, 2) for i in range(2)] + [outs[1]]


def dot_tn(left, right):
    return lax.dot_general(left, right, (((0,), (0,)), ((), ())), preferred_element_type=F32)


def feed_forward_kernel(blocked, devices, me_ref, count_ref, resid1_ref, cot_ref, vec_ref, *refs):
    pieces, refs = (refs[:10], refs[10:]) if blocked else (refs[:2], refs[2:])
    out_ref, g_resid1_ref, g_attn_ref, g_vec_ref = refs[:4]
    count = 4 if blocked else 2
    outs, refs = refs[4 : 4 + count], refs[4 + count :]
    made, refs = refs[:count], refs[count:]
    up, down, act, slope, low, acc, sems = refs
    rows, width = resid1_ref.shape
    blocks = up.shape[0]
    me = me_ref[0]
    share = width // devices
    long = share * blocks

    if blocked:
        for array, far, relative, top, bottom in piece_blocks(devices, 2 * long, long):
            piece = pieces[array].at[far]
            if bottom > long:
                row = pl.multiple_of((relative ^ me) * share, 8)
                for b in range(blocks):
                    pltpu.make_async_copy(
                        piece.at[pl.ds(long + b * share - top, share)],
                        up.at[b, pl.ds(row, share)],
                        sems.at[0],
                    ).start()
            if top == 0:
                row = pl.multiple_of((relative ^ me) * long, 8)
                pltpu.make_async_copy(
                    piece.at[pl.ds(0, long)], down.at[pl.ds(row, long)], sems.at[1]
                ).start()
    else:
        pltpu.make_async_copy(pieces[0], down, sems.at[1]).start()
        pltpu.make_async_copy(pieces[1], up, sems.at[0]).start()

    gain_one, shift_one, bdown, gain_two, shift_two = (vec_ref[i : i + 1, :] for i in range(3, 8))
    hidden1, normed1, inverse1 = layer_norm(resid1_ref[...], gain_one, shift_one)
    low[...] = hidden1.astype(BF16)
    acc[...] = hidden1 + bdown
    all_done(up, sems.at[0])

    def forward(b, carry):
        pre = dot_nn(low[...], up[b]) + vec_ref[pl.ds(8 + b, 1), :]
        cdf = 0.5 * (1.0 + lax.erf(pre * ROOT_HALF))
        slope[b] = cdf + pre * (jnp.exp(-0.5 * pre * pre) * INV_ROOT_TAU)
        activated = (pre * cdf).astype(BF16)
        if b == 0:
            all_done(down, sems.at[1])
        act[b] = activated
        acc[...] += dot_nn(activated, down[pl.ds(pl.multiple_of(b * width, width), width)])
        return carry

    for b in range(blocks):
        forward(b, 0)

    g_vec_ref[...] = jnp.zeros_like(g_vec_ref)
    result, normed2, inverse2 = layer_norm(acc[...], gain_two, shift_two)
    valid = lax.broadcasted_iota(jnp.int32, (rows, 1), 0) < count_ref[0]
    out_ref[...] = jnp.where(valid, result, 0.0).astype(BF16)
    g_out = jnp.where(valid, cot_ref[...].astype(F32), 0.0)
    g_vec_ref[6:7, :] = jnp.sum(g_out * normed2, axis=0, keepdims=True)
    g_vec_ref[7:8, :] = jnp.sum(g_out, axis=0, keepdims=True)
    g_resid2 = norm_back(g_out, normed2, inverse2, gain_two)
    acc[...] = g_resid2
    g_ffn = g_resid2.astype(BF16)
    g_vec_ref[5:6, :] = jnp.sum(g_ffn.astype(F32), axis=0, keepdims=True)

    def backward(b, carry):
        start = pl.multiple_of(b * width, width)
        down_b = down[pl.ds(start, width)]
        g_down = dot_tn(act[b], g_ffn).astype(BF16)
        if blocked:
            per = width // long // 2
            for i in range(per):
                pair = (g_down[(2 * i + j) * long : (2 * i + j + 1) * long] for j in range(2))
                index = (b * per + i) ^ (me >> 1)
                paired_store(pair, index, me & 1, *made[:2])
                for k in range(2):
                    pltpu.make_async_copy(
                        made[k].at[index], outs[k].at[index], sems.at[2 + k]
                    ).start()
        else:
            made[0][pl.ds(start, width)] = g_down
        g_pre = (dot_nt(g_ffn, down_b) * slope[b]).astype(BF16)
        g_vec_ref[pl.ds(8 + b, 1), :] = jnp.sum(g_pre.astype(F32), axis=0, keepdims=True)
        g_up = dot_tn(low[...], g_pre).astype(BF16)
        if blocked:
            for i in range(devices // 2):
                pair = (g_up[(2 * i + j) * share : (2 * i + j + 1) * share] for j in range(2))
                index = i ^ (me >> 1)
                paired_store(pair, (index, b), me & 1, *made[2:])
                for k in range(2, 4):
                    pltpu.make_async_copy(
                        made[k].at[index, b], outs[k].at[index, b], sems.at[2 + k]
                    ).start()
        else:
            made[1][b] = g_up
        acc[...] += dot_nt(g_pre, up[b])
        return carry

    for b in range(blocks):
        backward(b, 0)
    if not blocked:
        for k in range(2):
            pltpu.make_async_copy(made[k], outs[k], sems.at[2 + k]).start()
    g_hidden1 = acc[...]
    g_vec_ref[3:4, :] = jnp.sum(g_hidden1 * normed1, axis=0, keepdims=True)
    g_vec_ref[4:5, :] = jnp.sum(g_hidden1, axis=0, keepdims=True)
    g_resid1 = norm_back(g_hidden1, normed1, inverse1, gain_one)
    g_resid1_ref[...] = g_resid1
    g_attn = g_resid1.astype(BF16)
    g_attn_ref[...] = g_attn
    g_vec_ref[2:3, :] = jnp.sum(g_attn.astype(F32), axis=0, keepdims=True)
    for k in range(count):
        all_done(made[k], sems.at[2 + k])


def feed_forward(me, devices, hidden, count, resid1, cotangent, vectors, pieces):
    rows, width = resid1.shape
    share = width // devices
    blocks = hidden // width
    long = hidden // devices
    blocked = share % 8 == 0
    if blocked:
        g_shapes = [(devices // 2, long, width)] * 2 + [(devices // 2, blocks, share, width)] * 2
    else:
        rows_of = natural(pieces)
        up = rows_of[:, long:].reshape(devices, blocks, share, width).transpose(1, 0, 2, 3)
        pieces = (rows_of[:, :long].reshape(hidden, width), up.reshape(blocks, width, width))
        g_shapes = [(hidden, width), (blocks, width, width)]
    vmem = pl.BlockSpec(memory_space=pltpu.VMEM)
    smem = pl.BlockSpec(memory_space=pltpu.SMEM)
    any_space = pl.BlockSpec(memory_space=pl.ANY)
    outs = pl.pallas_call(
        partial(feed_forward_kernel, blocked, devices),
        in_specs=[smem, smem] + [vmem] * 3 + [any_space] * len(pieces),
        out_specs=[vmem] * 4 + [any_space] * len(g_shapes),
        out_shape=[
            jax.ShapeDtypeStruct((rows, width), BF16),
            jax.ShapeDtypeStruct((rows, width), F32),
            jax.ShapeDtypeStruct((rows, width), BF16),
            jax.ShapeDtypeStruct((16, width), F32),
        ]
        + [jax.ShapeDtypeStruct(shape, BF16) for shape in g_shapes],
        scratch_shapes=[pltpu.VMEM(shape, BF16) for shape in g_shapes]
        + [
            pltpu.VMEM((blocks, width, width), BF16),
            pltpu.VMEM((hidden, width), BF16),
            pltpu.VMEM((blocks, rows, width), BF16),
            pltpu.VMEM((blocks, rows, width), F32),
            pltpu.VMEM((rows, width), BF16),
            pltpu.VMEM((rows, width), F32),
            pltpu.SemaphoreType.DMA((6,)),
        ],
        compiler_params=pltpu.CompilerParams(vmem_limit_bytes=60 << 20),
        cost_estimate=pl.CostEstimate(
            flops=12 * rows * width * hidden,
            transcendentals=2 * rows * hidden,
            bytes_accessed=8 * width * hidden + 16 * rows * width,
        ),
    )(me, count, resid1, cotangent, vectors, *pieces)
    if blocked:
        return outs
    g_down = in_order(outs[4].reshape(devices, long, width))
    g_up = in_order(outs[5].reshape(blocks, devices, share, width).transpose(1, 0, 2, 3))
    pairs = [g.reshape((devices // 2, 2) + g.shape[1:]) for g in (g_down, g_up)]
    return list(outs[:4]) + [g[:, i] for g in pairs for i in range(2)]


def flip(array, stride):
    devices = lax.axis_size("dev")
    return lax.ppermute(array, "dev", [(i, i ^ stride) for i in range(devices)])


def gather_far(shard):
    blocks = [shard]
    for k in range(1, lax.axis_size("dev") // 8):
        low = k & -k
        blocks.append(flip(blocks[k - low], 8 * low))
    return blocks


def plane_neighbours(line):
    return flip(line, 2), flip(line, 4)


def plane_corner(across_x, across_y):
    return flip(across_x, 4), flip(across_y, 2)


def in_order(blocks):
    devices = blocks.shape[0]
    order = jnp.arange(devices, dtype=jnp.int32) ^ lax.axis_index("dev")
    return jnp.take(blocks, order, axis=0, mode="clip")


def add_low(left, right):
    return (left.astype(F32) + right.astype(F32)).astype(BF16)


def near_shape(block):
    return block.reshape((block.shape[0] // 4, 2, 2) + block.shape[1:])


def take(array, axis, index):
    return lax.index_in_dim(array, index, axis, keepdims=False)


def stage_sums(kept, got, axis):
    return tuple(add_low(take(kept, axis, i), take(got, axis, i)) for i in range(2))


def far_halves(part):
    pairs = part.reshape((part.shape[0] // 2, 2) + part.shape[1:])
    return pairs[:, 0], pairs[:, 1]


def scatter_far(part, stride, rows):
    while part.shape[0] > 1:
        keep, send = far_halves(part)
        got = flip(send, stride)
        if rows is not None:
            got, other = tied(got, flip(rows, stride))
            rows = rows + other
        part = add_low(keep, got) if part.shape[0] > 2 else keep.astype(F32) + got
        stride *= 2
    return part[0].astype(F32), rows


def tied(*values):
    return lax.optimization_barrier(values)


def shards(
    tokens,
    cotangent,
    lengths,
    dealing,
    w_query,
    w_key,
    w_value,
    w_out,
    b_query,
    b_value,
    b_out,
    norm1_gain,
    norm1_bias,
    w_up,
    b_up,
    w_down,
    b_down,
    norm2_gain,
    norm2_bias,
):
    devices = lax.axis_size("dev")
    me = lax.axis_index("dev")
    seq_count, local_len, width = tokens.shape
    per_device = seq_count // devices
    longest = local_len * devices
    capacity = cotangent.shape[0]
    share = w_query.shape[0]
    hidden = w_up.shape[1]

    outgoing = jnp.take(tokens, dealing, axis=0, mode="clip").reshape(devices, per_device, local_len, width)

    vectors = (
        b_query,
        b_value,
        b_out,
        norm1_gain,
        norm1_bias,
        b_down,
        norm2_gain,
        norm2_bias,
    )
    own_attn, own_ffn = prepare(
        me.reshape(1), (w_query, w_key, w_value, w_out), w_up, w_down, vectors, b_up
    )
    long = hidden // devices
    attn_line, ffn_line = gather_far(own_attn), gather_far(own_ffn)
    attn_line = jnp.stack(attn_line)
    attn_x, attn_y = plane_neighbours(attn_line)
    corner = attn_x[:, : 2 * share], attn_y[:, 2 * share :]
    outgoing, _, _, *ffn_line = tied(outgoing, *corner, *ffn_line)
    arrived = lax.all_to_all(outgoing, "dev", 0, 0)
    attn_own = (attn_line, attn_x, attn_y, *plane_corner(*corner))
    attn_pieces = (*attn_own, *(flip(block, 1) for block in attn_own))
    ffn_line = jnp.stack(ffn_line)
    ffn_x, ffn_y = plane_neighbours(ffn_line)

    my_slots = lax.dynamic_slice_in_dim(dealing, me * per_device, per_device)
    slot_len = jnp.take(lengths, my_slots)
    slot_ends = jnp.cumsum(slot_len)
    starts = slot_ends - slot_len
    row_ids = jnp.arange(capacity, dtype=jnp.int32)
    segment = jnp.sum((row_ids[:, None] >= slot_ends[None, :]).astype(jnp.int32), axis=1)
    is_valid = segment < per_device
    bounds = jnp.concatenate([starts, slot_ends[-1:]])
    picked = segment[:, None] == jnp.arange(per_device + 1, dtype=jnp.int32)[None, :]
    position = row_ids - jnp.sum(jnp.where(picked, bounds[None, :], 0), axis=1)
    source = (position // local_len) * (per_device * local_len) + segment * local_len
    source = jnp.where(is_valid, source + position % local_len, -1)

    packed, queries, key_rows, value_rows, vector_rows, weights = projections(
        me.reshape(1), devices, source, arrived.reshape(-1, width), attn_pieces
    )
    ffn_x, ffn_y, queries = tied(ffn_x, ffn_y, queries)
    corner = ffn_x[:, :long], ffn_y[:, long:]
    *corner, queries = tied(*corner, queries)
    ffn_corner = plane_corner(*corner)
    context, log_total, resid1 = attention_forward(
        segment, packed, vector_rows, queries, key_rows, value_rows, weights
    )
    *ffn_corner, resid1 = tied(*ffn_corner, resid1)
    ffn_own = (ffn_line, ffn_x, ffn_y, *ffn_corner)
    ffn_pieces = (*ffn_own, *(flip(block, 1) for block in ffn_own))

    layer_out, g_resid1, g_attn, g_rows, a_keep, a_send, b_keep, b_send = feed_forward(
        me.reshape(1), devices, hidden, slot_ends[-1:], resid1, cotangent, vector_rows, ffn_pieces
    )

    col_blocks = hidden // width
    own_far = devices // 8

    got_a, got_b = flip(a_send, 1), flip(b_send, 1)
    backward = partial(attention_backward, segment=segment, log_total=log_total, weights=weights)
    operands = dict(queries=queries, key_rows=key_rows, value_rows=value_rows)
    grads_0 = backward(0, 1, g_attn=g_attn, **operands)
    got_a, got_b, *grads_0 = tied(got_a, got_b, *grads_0)
    a_keep, a_send = stage_sums(near_shape(a_keep), near_shape(got_a), 2)
    b_keep, b_send = stage_sums(near_shape(b_keep), near_shape(got_b), 1)
    a_send, b_send, g_attn_late = tied(a_send, b_send, g_attn)
    got_a, got_b = flip(a_send, 2), flip(b_send, 4)
    grads_1 = backward(1, width // GROUP, g_attn=g_attn_late, **operands)
    step_ids = jnp.arange(longest, dtype=jnp.int32).reshape(devices, 1, local_len)
    inside = step_ids < slot_len[None, :, None]
    take_rows = jnp.where(inside, starts[None, :, None] + step_ids, -1).reshape(-1)
    gradients = (grads_0, grads_1)
    unpacked = input_gradient(take_rows, g_resid1, weights, gradients)
    got_a, got_b, unpacked, g_attn_late, *grads_1 = tied(
        got_a, got_b, unpacked, g_attn_late, *grads_1
    )
    returned = lax.all_to_all(
        unpacked.reshape(devices, per_device, local_len, width), "dev", 0, 0
    )
    a_keep, a_send = stage_sums(a_keep, got_a, 1)
    b_keep, b_send = stage_sums(b_keep, got_b, 1)
    got_a, got_b = flip(a_send, 4), flip(b_send, 2)

    c_keep, c_send, d_keep, d_send, g_rows_attn = weight_gradients(
        me.reshape(1), devices, packed, context, g_attn_late, (grads_0, grads_1)
    )
    g_rows = g_rows + jnp.pad(g_rows_attn, ((0, 8), (0, 0)))
    got_a, got_b, got_c, got_d, g_other = tied(
        got_a, got_b, flip(c_send, 1), flip(d_send, 1), flip(g_rows, 1)
    )
    ffn_part = jnp.concatenate(
        [
            add_low(a_keep, got_a),
            add_low(b_keep, got_b).reshape(own_far, -1, width),
        ],
        axis=1,
    )
    ffn_keep, ffn_send = far_halves(ffn_part)
    ffn_got = flip(ffn_send, 8)
    c_keep, c_send = stage_sums(near_shape(c_keep), near_shape(got_c), 2)
    d_keep, d_send = stage_sums(near_shape(d_keep), near_shape(got_d), 1)
    g_rows = g_rows + g_other
    got_c, got_d, g_other = tied(flip(c_send, 2), flip(d_send, 4), flip(g_rows, 2))
    c_keep, c_send = stage_sums(c_keep, got_c, 1)
    d_keep, d_send = stage_sums(d_keep, got_d, 1)
    g_rows = g_rows + g_other
    ffn_got, got_c, got_d, g_other, returned = tied(
        ffn_got, flip(c_send, 4), flip(d_send, 2), flip(g_rows, 4), returned
    )
    ffn_part = add_low(ffn_keep, ffn_got)
    attn_part = jnp.concatenate([add_low(c_keep, got_c), add_low(d_keep, got_d)], axis=1)
    g_rows = g_rows + g_other
    attn_keep, attn_send = far_halves(attn_part)
    attn_got, g_other = tied(flip(attn_send, 8), flip(g_rows, 8))
    attn_part = add_low(attn_keep, attn_got)
    g_rows = g_rows + g_other
    ffn_sum, _ = scatter_far(ffn_part, 16, None)
    attn_sum, g_rows = scatter_far(attn_part, 16, g_rows)
    g_wdown = ffn_sum[:long]
    g_wup = ffn_sum[long:].reshape(col_blocks, share, width)
    g_wup = g_wup.transpose(1, 0, 2).reshape(share, hidden)
    own_vec = lax.dynamic_slice_in_dim(g_rows[:8], me * share, share, axis=1)
    up_rows = g_rows[8 : 8 + col_blocks].reshape(hidden)
    own_up = lax.dynamic_slice_in_dim(up_rows, me * (hidden // devices), hidden // devices)

    slots = jnp.arange(seq_count, dtype=jnp.int32)
    inverse_deal = jnp.sum(jnp.where(dealing[None, :] == slots[:, None], slots[None, :], 0), axis=1)
    returned = returned.reshape(seq_count, local_len, width)
    input_grad = jnp.take(returned, inverse_deal, axis=0, mode="clip")
    return (
        layer_out,
        input_grad,
        attn_sum[0],
        attn_sum[1],
        attn_sum[2],
        attn_sum[3],
        own_vec[0],
        own_vec[1],
        own_vec[2],
        own_vec[3],
        own_vec[4],
        g_wup,
        own_up,
        g_wdown,
        own_vec[5],
        own_vec[6],
        own_vec[7],
    )


def solution(mesh):
    rows = P("dev", None)
    vector = P("dev")
    seqs = P(None, "dev", None)
    return jax.shard_map(
        shards,
        mesh=mesh,
        in_specs=(
            (seqs, rows, P(), P())
            + (rows,) * 4
            + (vector,) * 5
            + (rows, vector, rows)
            + (vector,) * 3
        ),
        out_specs=(
            (rows, seqs) + (rows,) * 4 + (vector,) * 5 + (rows, vector, rows) + (vector,) * 3
        ),
        check_vma=False,
    )
```

```python
from functools import partial

import jax
import jax.numpy as jnp
from jax import lax
from jax.experimental import pallas as pl
from jax.experimental.pallas import tpu as pltpu
from jax.sharding import PartitionSpec as P

HEADS = 12
HEAD_DIM = 64
PAIR = 2 * HEAD_DIM
GROUP = 4 * HEAD_DIM

MASKED_SCORE = -1e30
ROOT_HALF = 0.7071067811865476
INV_ROOT_TAU = 0.3989422804014327
BF16 = jnp.bfloat16
F32 = jnp.float32


def layer_norm(residual, norm_gain, norm_shift):
    center = residual - jnp.mean(residual, axis=-1, keepdims=True)
    inverse = lax.rsqrt(jnp.mean(center * center, axis=-1, keepdims=True) + 1e-05)
    normed = center * inverse
    return (normed * norm_gain + norm_shift, normed, inverse)


def norm_back(upstream, normed, inverse, norm_gain):
    scaled = upstream * norm_gain
    return inverse * (
        scaled
        - jnp.mean(scaled, axis=-1, keepdims=True)
        - normed * jnp.mean(scaled * normed, axis=-1, keepdims=True)
    )


def dot_nt(left, right):
    return lax.dot_general(left, right, (((1,), (1,)), ((), ())), preferred_element_type=F32)


def dot_nn(left, right):
    return lax.dot_general(left, right, (((1,), (0,)), ((), ())), preferred_element_type=F32)


def piece_blocks(devices, height, split):
    for core in range(2):
        for far in range(devices // 8):
            for near in range(4):
                relative = core + 2 * near + 8 * far
                if near < 3:
                    yield 5 * core + near, far, relative, 0, height
                else:
                    yield 5 * core + 3, far, relative, 0, split
                    yield 5 * core + 4, far, relative, split, height


def all_done(ref, sem):
    pltpu.make_async_copy(ref, ref, sem).wait()


def prepare_kernel(me_ref, *refs):
    weights, up_ref, down_ref, vectors, b_up = refs[:4], refs[4], refs[5], refs[6:14], refs[14]
    attn_ref, ffn_ref, rows_ref = refs[15:]
    share, width = weights[0].shape
    long = b_up.shape[1]
    me = me_ref[0]
    for i, weight in enumerate(weights):
        attn_ref[i * share : (i + 1) * share] = weight[...]
    ffn_ref[:long] = down_ref[...]
    for b in range(long // share):
        row = long + b * share
        ffn_ref[row : row + share] = up_ref[:, b * width : (b + 1) * width]
    rows_ref[...] = jnp.zeros_like(rows_ref)
    for i, vector in enumerate(vectors):
        rows_ref[i : i + 1, 0:share] = vector[...].astype(F32)
    for i in range(8, 16):
        rows_ref[i : i + 1, 0:long] = b_up[...].astype(F32)
    values = rows_ref[...].astype(BF16)
    shape = (values.shape[1], width)
    source = lax.broadcasted_iota(jnp.int32, shape, 0)
    target = lax.broadcasted_iota(jnp.int32, shape, 1)
    moved = []
    for start in (me * share, (me * long) % width):
        here = jnp.where(target == source + start, 1.0, 0.0).astype(BF16)
        moved.append(dot_nn(values, here))
    row = lax.broadcasted_iota(jnp.int32, moved[0].shape, 0)
    of_up = jnp.where(row == 8 + (me * long) // width, moved[1], 0.0)
    attn_ref[4 * share :] = jnp.where(row < 8, moved[0], of_up).astype(BF16)


def prepare(me, weights, w_up, w_down, vectors, b_up):
    share, width = weights[0].shape
    long = w_down.shape[0]
    vmem = pl.BlockSpec(memory_space=pltpu.VMEM)
    smem = pl.BlockSpec(memory_space=pltpu.SMEM)
    rows = [vector.reshape(1, -1) for vector in vectors + (b_up,)]
    return pl.pallas_call(
        prepare_kernel,
        in_specs=[smem] + [vmem] * 15,
        out_specs=[vmem] * 2,
        out_shape=[
            jax.ShapeDtypeStruct((4 * share + 16, width), BF16),
            jax.ShapeDtypeStruct((2 * long, width), BF16),
        ],
        scratch_shapes=[pltpu.VMEM((16, PAIR), F32)],
        cost_estimate=pl.CostEstimate(flops=1 << 22, transcendentals=0, bytes_accessed=1 << 20),
    )(me, *weights, w_up, w_down, *rows)


def projection_kernel(blocked, devices, me_ref, source_ref, arrived_ref, *refs):
    pieces, refs = (refs[:10], refs[10:]) if blocked else (refs[:2], refs[2:])
    packed_ref, q_ref, k_ref, v_ref, vec_ref, w_out_ref, weights, vec_rows, sems = refs
    rows, width = packed_ref.shape
    share = width // devices
    me = me_ref[0]
    if blocked:
        height = 4 * share + 16
        for array, far, relative, top, bottom in piece_blocks(devices, height, 2 * share):
            row = pl.multiple_of((relative ^ me) * share, 8)
            for i in range(top // share, min(bottom // share, 4)):
                pltpu.make_async_copy(
                    pieces[array].at[far, pl.ds(i * share - top, share)],
                    weights.at[i, pl.ds(row, share)],
                    sems.at[0],
                ).start()
            if bottom == height:
                pltpu.make_async_copy(
                    pieces[array].at[far, pl.ds(4 * share - top, 16)],
                    vec_rows.at[relative],
                    sems.at[1],
                ).start()
    else:
        pltpu.make_async_copy(pieces[0], weights, sems.at[0]).start()
        pltpu.make_async_copy(pieces[1], vec_rows, sems.at[1]).start()
    places = arrived_ref.shape[0]
    block = rows // 4
    for i in range(4):
        here = slice(i * block, (i + 1) * block)
        pick = source_ref[here] == lax.broadcasted_iota(jnp.int32, (block, places), 1)
        pick = jnp.where(pick, 1.0, 0.0).astype(BF16)
        packed_ref[here] = dot_nn(pick, arrived_ref[...]).astype(BF16)
    all_done(vec_rows, sems.at[1])
    vec_ref[...] = jnp.sum(vec_rows[...].astype(F32), axis=0)
    all_done(weights, sems.at[0])
    out_copy = pltpu.make_async_copy(weights, w_out_ref, sems.at[2])
    out_copy.start()
    packed = packed_ref[...]
    q_ref[...] = ((dot_nn(packed, weights[0]) + vec_ref[0:1, :]) * 0.125).astype(BF16)
    k_ref[...] = dot_nn(packed, weights[1]).astype(BF16)
    v_ref[...] = (dot_nn(packed, weights[2]) + vec_ref[1:2, :]).astype(BF16)
    out_copy.wait()


def attention_forward_kernel(
    seg_col, seg_row, packed_ref, vec_ref, q_ref, k_ref, v_ref, wo_ref, ctx_ref, lse_ref, resid_ref, bias
):
    step = pl.program_id(0)
    rows = q_ref.shape[0]

    @pl.when(step == 0)
    def _():
        bias[...] = jnp.where(seg_col[...] == seg_row[...], 0.0, MASKED_SCORE)
        resid_ref[...] = packed_ref[...].astype(F32) + vec_ref[2:3, :]

    lane = lax.broadcasted_iota(jnp.int32, (rows, PAIR), 1)
    stats = lse_ref[...]
    for pair in range(GROUP // PAIR):
        span = slice(pair * PAIR, (pair + 1) * PAIR)
        q_pair, k_pair, v_pair = q_ref[:, span], k_ref[:, span], v_ref[:, span]
        outs = []
        for half in range(2):
            own = (lane // HEAD_DIM) == half
            q_own = jnp.where(own, q_pair, jnp.zeros_like(q_pair))
            scores = dot_nt(q_own, k_pair) + bias[...]
            top = jnp.max(scores, axis=1, keepdims=True)
            exped = jnp.exp(scores - top)
            total = jnp.sum(exped, axis=1, keepdims=True)
            outs.append(dot_nn(exped.astype(BF16), v_pair) * (1.0 / total))
            head = step * (GROUP // HEAD_DIM) + pair * 2 + half
            stats = jnp.where(lane == head, top + jnp.log(total), stats)
        ctx_ref[:, span] = jnp.where(lane < HEAD_DIM, outs[0], outs[1]).astype(BF16)
    lse_ref[...] = stats
    resid_ref[...] += dot_nn(ctx_ref[...], wo_ref[...])


def natural(pieces):
    corners = [jnp.concatenate(pieces[i + 3 : i + 5], axis=1) for i in (0, 5)]
    blocks = jnp.stack(
        [b for i, corner in zip((0, 5), corners) for b in (*pieces[i : i + 3], corner)], axis=1
    )
    far = blocks.shape[0]
    blocks = blocks.reshape((far, 2, 4) + blocks.shape[2:]).swapaxes(1, 2)
    return in_order(blocks.reshape((8 * far,) + blocks.shape[3:]))


def projections(me, devices, source, arrived, pieces):
    rows, width = source.shape[0], arrived.shape[1]
    share = width // devices
    blocked = share % 8 == 0
    if not blocked:
        rows_of = natural(pieces)
        parts = [rows_of[:, i * share : (i + 1) * share].reshape(width, width) for i in range(4)]
        pieces = (jnp.stack(parts), rows_of[:, 4 * share :])
    vmem = pl.BlockSpec(memory_space=pltpu.VMEM)
    any_space = pl.BlockSpec(memory_space=pl.ANY)
    return pl.pallas_call(
        partial(projection_kernel, blocked, devices),
        in_specs=[pl.BlockSpec(memory_space=pltpu.SMEM), vmem, vmem] + [any_space] * len(pieces),
        out_specs=[vmem] * 5 + [any_space],
        out_shape=[jax.ShapeDtypeStruct((rows, width), BF16)] * 4
        + [
            jax.ShapeDtypeStruct((16, width), F32),
            jax.ShapeDtypeStruct((4, width, width), BF16),
        ],
        scratch_shapes=[
            pltpu.VMEM((4, width, width), BF16),
            pltpu.VMEM((devices, 16, width), BF16),
            pltpu.SemaphoreType.DMA((3,)),
        ],
        compiler_params=pltpu.CompilerParams(vmem_limit_bytes=40 << 20),
        cost_estimate=pl.CostEstimate(
            flops=6 * rows * width * width + 2 * rows * width * arrived.shape[0],
            transcendentals=0,
            bytes_accessed=16 * width * width + rows * width * 10,
        ),
    )(me, source[:, None], arrived, *pieces)


def attention_forward(segment, packed, vectors, queries, key_rows, value_rows, weights):
    rows, width = packed.shape
    block = pl.BlockSpec((rows, GROUP), lambda g: (0, g))
    whole = lambda shape: pl.BlockSpec(shape, lambda g: (0, 0))
    return pl.pallas_call(
        attention_forward_kernel,
        grid=(width // GROUP,),
        in_specs=[
            whole((rows, 1)),
            whole((1, rows)),
            whole((rows, width)),
            whole((16, width)),
            block,
            block,
            block,
            pl.BlockSpec((None, GROUP, width), lambda g: (3, g, 0)),
        ],
        out_specs=[block, whole((rows, PAIR)), whole((rows, width))],
        out_shape=[
            jax.ShapeDtypeStruct((rows, width), BF16),
            jax.ShapeDtypeStruct((rows, PAIR), F32),
            jax.ShapeDtypeStruct((rows, width), F32),
        ],
        scratch_shapes=[pltpu.VMEM((rows, rows), F32)],
        compiler_params=pltpu.CompilerParams(vmem_limit_bytes=48 << 20),
        cost_estimate=pl.CostEstimate(
            flops=HEADS * rows * rows * PAIR * 4 + 2 * rows * width * width,
            transcendentals=HEADS * rows * rows,
            bytes_accessed=2 * width * width + rows * width * 14,
        ),
    )(
        segment[:, None],
        segment[None, :],
        packed,
        vectors,
        queries,
        key_rows,
        value_rows,
        weights,
    )


def attention_backward_kernel(
    first,
    seg_col,
    seg_row,
    lse_ref,
    g_attn_ref,
    w_out_ref,
    q_ref,
    k_ref,
    v_ref,
    dq_ref,
    dk_ref,
    dv_ref,
    bias,
):
    step = pl.program_id(0)

    @pl.when(step == 0)
    def _():
        bias[...] = jnp.where(seg_col[...] == seg_row[...], 0.0, MASKED_SCORE)

    rows = q_ref.shape[0]
    lane = lax.broadcasted_iota(jnp.int32, (rows, PAIR), 1)
    g_context = dot_nt(g_attn_ref[...], w_out_ref[...]).astype(BF16)
    for pair in range(GROUP // PAIR):
        span = slice(pair * PAIR, (pair + 1) * PAIR)
        q_pair, k_pair, v_pair = q_ref[:, span], k_ref[:, span], v_ref[:, span]
        g_pair = g_context[:, span]
        q_turn, g_turn = q_pair.T, g_pair.T
        dq, dk, dv = [], [], []
        for half in range(2):
            own = (lane // HEAD_DIM) == half
            part = slice(half * HEAD_DIM, (half + 1) * HEAD_DIM)
            zero = jnp.zeros_like(q_pair)
            head = (first + step) * (GROUP // HEAD_DIM) + pair * 2 + half
            log_total = jnp.sum(jnp.where(lane == head, lse_ref[...], 0.0), axis=1, keepdims=True)
            scores = dot_nt(jnp.where(own, q_pair, zero), k_pair) + bias[...]
            probs = jnp.exp(scores - log_total)
            low = probs.astype(BF16)
            g_probs = dot_nt(jnp.where(own, g_pair, zero), v_pair)
            product = probs * g_probs
            g_scores = (product - probs * jnp.sum(product, axis=1, keepdims=True)).astype(BF16)
            dq.append(dot_nn(g_scores, k_pair))
            dk.append(dot_nn(q_turn[part], g_scores))
            dv.append(dot_nn(g_turn[part], low))
        dq_ref[:, span] = jnp.where(lane < HEAD_DIM, dq[0], dq[1]).astype(BF16)
        dk_ref[:, span] = jnp.concatenate(dk, axis=0).T.astype(BF16)
        dv_ref[:, span] = jnp.concatenate(dv, axis=0).T.astype(BF16)


def attention_backward(first, last, segment, log_total, g_attn, weights, queries, key_rows, value_rows):
    rows, width = queries.shape
    taken = pl.BlockSpec((rows, GROUP), lambda g: (0, g + first))
    made = pl.BlockSpec((rows, GROUP), lambda g: (0, g))
    whole = lambda shape: pl.BlockSpec(shape, lambda g: (0, 0))
    count = last - first
    return pl.pallas_call(
        partial(attention_backward_kernel, first),
        grid=(count,),
        in_specs=[
            whole((rows, 1)),
            whole((1, rows)),
            whole((rows, PAIR)),
            whole((rows, width)),
            pl.BlockSpec((None, GROUP, width), lambda g: (3, g + first, 0)),
        ]
        + [taken] * 3,
        out_specs=[made] * 3,
        out_shape=[jax.ShapeDtypeStruct((rows, count * GROUP), BF16)] * 3,
        scratch_shapes=[pltpu.VMEM((rows, rows), F32)],
        compiler_params=pltpu.CompilerParams(vmem_limit_bytes=48 << 20),
        cost_estimate=pl.CostEstimate(
            flops=count * 4 * rows * rows * PAIR * 10,
            transcendentals=count * 4 * rows * rows,
            bytes_accessed=count * rows * GROUP * 14,
        ),
    )(segment[:, None], segment[None, :], log_total, g_attn, weights, queries, key_rows, value_rows)


def input_gradient_kernel(parts, row_ref, resid_ref, w_ref, *refs):
    out_ref = refs[-1]
    rows = resid_ref.shape[0]
    total = resid_ref[...]
    column = 0
    for i in range(parts):
        dq, dk, dv = (refs[3 * i + j] for j in range(3))
        span = slice(column, column + dq.shape[1])
        column += dq.shape[1]
        total += dot_nt(dq[...], w_ref[0, :, span]) * 0.125
        total += dot_nt(dk[...], w_ref[1, :, span])
        total += dot_nt(dv[...], w_ref[2, :, span])
    g_input = total.astype(BF16)
    places = row_ref.shape[0]
    block = places // 4
    for i in range(4):
        here = slice(i * block, (i + 1) * block)
        pick = row_ref[here] == lax.broadcasted_iota(jnp.int32, (block, rows), 1)
        pick = jnp.where(pick, 1.0, 0.0).astype(BF16)
        out_ref[here] = dot_nn(pick, g_input).astype(BF16)


def input_gradient(take_rows, g_resid1, weights, gradients):
    rows, width = g_resid1.shape
    places = take_rows.shape[0]
    flat = [g for group in gradients for g in group]
    vmem = pl.BlockSpec(memory_space=pltpu.VMEM)
    return pl.pallas_call(
        partial(input_gradient_kernel, len(gradients)),
        in_specs=[vmem] * (3 + len(flat)),
        out_specs=vmem,
        out_shape=jax.ShapeDtypeStruct((places, width), BF16),
        compiler_params=pltpu.CompilerParams(vmem_limit_bytes=48 << 20),
        cost_estimate=pl.CostEstimate(
            flops=6 * rows * width * width + 2 * places * rows * width,
            transcendentals=0,
            bytes_accessed=12 * width * width + 10 * rows * width + 2 * places * width,
        ),
    )(take_rows[:, None], g_resid1, weights, *flat)


def paired_store(values, index, core, keep_ref, send_ref):
    low, high = values
    first = core == 0
    keep_ref[index] = jnp.where(first, low, high)
    send_ref[index] = jnp.where(first, high, low)


def weight_gradient_kernel(blocked, parts, me_ref, x_ref, ctx_ref, g_attn_ref, *refs):
    ins, outs = refs[: 3 * parts], refs[3 * parts :]
    rows, width = x_ref.shape
    me = me_ref[0]
    core = me & 1
    vec_ref = outs[-1]
    vec_ref[...] = jnp.zeros_like(vec_ref)

    def store(kind, grad):
        if not blocked:
            outs[0][kind] = grad
            return
        keep, send = (outs[2 * (kind // 2) + i] for i in range(2))
        share = keep.shape[2]
        for i in range(keep.shape[0]):
            low, high = (grad[(2 * i + j) * share : (2 * i + j + 1) * share] for j in range(2))
            paired_store((low, high), (i ^ (me >> 1), kind % 2), core, keep, send)

    x_turn = x_ref[...].T
    for j in range(3):
        pieces = []
        for i in range(parts):
            grads = ins[3 * i + j][...]
            span = slice(i * grads.shape[1], (i + 1) * grads.shape[1])
            piece = dot_nn(x_turn, grads)
            pieces.append((piece * 0.125 if j == 0 else piece).astype(BF16))
        store(j, jnp.concatenate(pieces, axis=1))
    store(3, dot_tn(ctx_ref[...], g_attn_ref[...]).astype(BF16))
    column = 0
    for i in range(parts):
        dq, _, dv = (ins[3 * i + j][...].astype(F32) for j in range(3))
        span = slice(column, column + dq.shape[1])
        column += dq.shape[1]
        vec_ref[0:1, span] = jnp.sum(dq, axis=0, keepdims=True) * 0.125
        vec_ref[1:2, span] = jnp.sum(dv, axis=0, keepdims=True)


def weight_gradients(me, devices, packed, context, g_attn, gradients):
    rows, width = packed.shape
    share = width // devices
    blocked = share % 8 == 0
    flat = [g for group in gradients for g in group]
    vmem = pl.BlockSpec(memory_space=pltpu.VMEM)
    smem = pl.BlockSpec(memory_space=pltpu.SMEM)
    if blocked:
        shapes = [jax.ShapeDtypeStruct((devices // 2, 2, share, width), BF16)] * 4
    else:
        shapes = [jax.ShapeDtypeStruct((4, width, width), BF16)]
    shapes.append(jax.ShapeDtypeStruct((8, width), F32))
    outs = pl.pallas_call(
        partial(weight_gradient_kernel, blocked, len(gradients)),
        in_specs=[smem] + [vmem] * (3 + len(flat)),
        out_specs=[vmem] * len(shapes),
        out_shape=shapes,
        compiler_params=pltpu.CompilerParams(vmem_limit_bytes=48 << 20),
        cost_estimate=pl.CostEstimate(
            flops=8 * rows * width * width,
            transcendentals=0,
            bytes_accessed=8 * width * width + 12 * rows * width,
        ),
    )(me, packed, context, g_attn, *flat)
    if blocked:
        return outs
    grads = in_order(outs[0].reshape(4, devices, share, width).transpose(1, 0, 2, 3))
    grads = grads.reshape(devices // 2, 2, 4, share, width)
    return [grads[:, i, j : j + 2] for j in (0, 2) for i in range(2)] + [outs[1]]


def dot_tn(left, right):
    return lax.dot_general(left, right, (((0,), (0,)), ((), ())), preferred_element_type=F32)


def feed_forward_kernel(blocked, devices, me_ref, count_ref, resid1_ref, cot_ref, vec_ref, *refs):
    pieces, refs = (refs[:10], refs[10:]) if blocked else (refs[:2], refs[2:])
    out_ref, g_resid1_ref, g_attn_ref, g_vec_ref = refs[:4]
    count = 4 if blocked else 2
    outs, refs = refs[4 : 4 + count], refs[4 + count :]
    made, refs = refs[:count], refs[count:]
    up, down, act, slope, low, acc, sems = refs
    rows, width = resid1_ref.shape
    blocks = up.shape[0]
    me = me_ref[0]
    share = width // devices
    long = share * blocks

    if blocked:
        for array, far, relative, top, bottom in piece_blocks(devices, 2 * long, long):
            piece = pieces[array].at[far]
            if bottom > long:
                row = pl.multiple_of((relative ^ me) * share, 8)
                for b in range(blocks):
                    pltpu.make_async_copy(
                        piece.at[pl.ds(long + b * share - top, share)],
                        up.at[b, pl.ds(row, share)],
                        sems.at[0],
                    ).start()
            if top == 0:
                row = pl.multiple_of((relative ^ me) * long, 8)
                pltpu.make_async_copy(
                    piece.at[pl.ds(0, long)], down.at[pl.ds(row, long)], sems.at[1]
                ).start()
    else:
        pltpu.make_async_copy(pieces[0], down, sems.at[1]).start()
        pltpu.make_async_copy(pieces[1], up, sems.at[0]).start()

    gain_one, shift_one, bdown, gain_two, shift_two = (vec_ref[i : i + 1, :] for i in range(3, 8))
    hidden1, normed1, inverse1 = layer_norm(resid1_ref[...], gain_one, shift_one)
    low[...] = hidden1.astype(BF16)
    acc[...] = hidden1 + bdown
    all_done(up, sems.at[0])

    def forward(b, carry):
        pre = dot_nn(low[...], up[b]) + vec_ref[pl.ds(8 + b, 1), :]
        cdf = 0.5 * (1.0 + lax.erf(pre * ROOT_HALF))
        slope[b] = cdf + pre * (jnp.exp(-0.5 * pre * pre) * INV_ROOT_TAU)
        activated = (pre * cdf).astype(BF16)
        if b == 0:
            all_done(down, sems.at[1])
        act[b] = activated
        acc[...] += dot_nn(activated, down[pl.ds(pl.multiple_of(b * width, width), width)])
        return carry

    for b in range(blocks):
        forward(b, 0)

    g_vec_ref[...] = jnp.zeros_like(g_vec_ref)
    result, normed2, inverse2 = layer_norm(acc[...], gain_two, shift_two)
    valid = lax.broadcasted_iota(jnp.int32, (rows, 1), 0) < count_ref[0]
    out_ref[...] = jnp.where(valid, result, 0.0).astype(BF16)
    g_out = jnp.where(valid, cot_ref[...].astype(F32), 0.0)
    g_vec_ref[6:7, :] = jnp.sum(g_out * normed2, axis=0, keepdims=True)
    g_vec_ref[7:8, :] = jnp.sum(g_out, axis=0, keepdims=True)
    g_resid2 = norm_back(g_out, normed2, inverse2, gain_two)
    acc[...] = g_resid2
    g_ffn = g_resid2.astype(BF16)
    g_vec_ref[5:6, :] = jnp.sum(g_ffn.astype(F32), axis=0, keepdims=True)

    def backward(b, carry):
        start = pl.multiple_of(b * width, width)
        down_b = down[pl.ds(start, width)]
        g_down = dot_tn(act[b], g_ffn).astype(BF16)
        if blocked:
            per = width // long // 2
            for i in range(per):
                pair = (g_down[(2 * i + j) * long : (2 * i + j + 1) * long] for j in range(2))
                index = (b * per + i) ^ (me >> 1)
                paired_store(pair, index, me & 1, *made[:2])
                for k in range(2):
                    pltpu.make_async_copy(
                        made[k].at[index], outs[k].at[index], sems.at[2 + k]
                    ).start()
        else:
            made[0][pl.ds(start, width)] = g_down
        g_pre = (dot_nt(g_ffn, down_b) * slope[b]).astype(BF16)
        g_vec_ref[pl.ds(8 + b, 1), :] = jnp.sum(g_pre.astype(F32), axis=0, keepdims=True)
        g_up = dot_tn(low[...], g_pre).astype(BF16)
        if blocked:
            for i in range(devices // 2):
                pair = (g_up[(2 * i + j) * share : (2 * i + j + 1) * share] for j in range(2))
                index = i ^ (me >> 1)
                paired_store(pair, (index, b), me & 1, *made[2:])
                for k in range(2, 4):
                    pltpu.make_async_copy(
                        made[k].at[index, b], outs[k].at[index, b], sems.at[2 + k]
                    ).start()
        else:
            made[1][b] = g_up
        acc[...] += dot_nt(g_pre, up[b])
        return carry

    for b in range(blocks):
        backward(b, 0)
    if not blocked:
        for k in range(2):
            pltpu.make_async_copy(made[k], outs[k], sems.at[2 + k]).start()
    g_hidden1 = acc[...]
    g_vec_ref[3:4, :] = jnp.sum(g_hidden1 * normed1, axis=0, keepdims=True)
    g_vec_ref[4:5, :] = jnp.sum(g_hidden1, axis=0, keepdims=True)
    g_resid1 = norm_back(g_hidden1, normed1, inverse1, gain_one)
    g_resid1_ref[...] = g_resid1
    g_attn = g_resid1.astype(BF16)
    g_attn_ref[...] = g_attn
    g_vec_ref[2:3, :] = jnp.sum(g_attn.astype(F32), axis=0, keepdims=True)
    for k in range(count):
        all_done(made[k], sems.at[2 + k])


def feed_forward(me, devices, hidden, count, resid1, cotangent, vectors, pieces):
    rows, width = resid1.shape
    share = width // devices
    blocks = hidden // width
    long = hidden // devices
    blocked = share % 8 == 0
    if blocked:
        g_shapes = [(devices // 2, long, width)] * 2 + [(devices // 2, blocks, share, width)] * 2
    else:
        rows_of = natural(pieces)
        up = rows_of[:, long:].reshape(devices, blocks, share, width).transpose(1, 0, 2, 3)
        pieces = (rows_of[:, :long].reshape(hidden, width), up.reshape(blocks, width, width))
        g_shapes = [(hidden, width), (blocks, width, width)]
    vmem = pl.BlockSpec(memory_space=pltpu.VMEM)
    smem = pl.BlockSpec(memory_space=pltpu.SMEM)
    any_space = pl.BlockSpec(memory_space=pl.ANY)
    outs = pl.pallas_call(
        partial(feed_forward_kernel, blocked, devices),
        in_specs=[smem, smem] + [vmem] * 3 + [any_space] * len(pieces),
        out_specs=[vmem] * 4 + [any_space] * len(g_shapes),
        out_shape=[
            jax.ShapeDtypeStruct((rows, width), BF16),
            jax.ShapeDtypeStruct((rows, width), F32),
            jax.ShapeDtypeStruct((rows, width), BF16),
            jax.ShapeDtypeStruct((16, width), F32),
        ]
        + [jax.ShapeDtypeStruct(shape, BF16) for shape in g_shapes],
        scratch_shapes=[pltpu.VMEM(shape, BF16) for shape in g_shapes]
        + [
            pltpu.VMEM((blocks, width, width), BF16),
            pltpu.VMEM((hidden, width), BF16),
            pltpu.VMEM((blocks, rows, width), BF16),
            pltpu.VMEM((blocks, rows, width), F32),
            pltpu.VMEM((rows, width), BF16),
            pltpu.VMEM((rows, width), F32),
            pltpu.SemaphoreType.DMA((6,)),
        ],
        compiler_params=pltpu.CompilerParams(vmem_limit_bytes=60 << 20),
        cost_estimate=pl.CostEstimate(
            flops=12 * rows * width * hidden,
            transcendentals=2 * rows * hidden,
            bytes_accessed=8 * width * hidden + 16 * rows * width,
        ),
    )(me, count, resid1, cotangent, vectors, *pieces)
    if blocked:
        return outs
    g_down = in_order(outs[4].reshape(devices, long, width))
    g_up = in_order(outs[5].reshape(blocks, devices, share, width).transpose(1, 0, 2, 3))
    pairs = [g.reshape((devices // 2, 2) + g.shape[1:]) for g in (g_down, g_up)]
    return list(outs[:4]) + [g[:, i] for g in pairs for i in range(2)]


def flip(array, stride):
    devices = lax.axis_size("dev")
    return lax.ppermute(array, "dev", [(i, i ^ stride) for i in range(devices)])


def gather_far(shard):
    blocks = [shard]
    for k in range(1, lax.axis_size("dev") // 8):
        low = k & -k
        blocks.append(flip(blocks[k - low], 8 * low))
    return blocks


def plane_neighbours(line):
    return flip(line, 2), flip(line, 4)


def plane_corner(across_x, across_y):
    return flip(across_x, 4), flip(across_y, 2)


def in_order(blocks):
    devices = blocks.shape[0]
    order = jnp.arange(devices, dtype=jnp.int32) ^ lax.axis_index("dev")
    return jnp.take(blocks, order, axis=0, mode="clip")


def add_low(left, right):
    return (left.astype(F32) + right.astype(F32)).astype(BF16)


def near_shape(block):
    return block.reshape((block.shape[0] // 4, 2, 2) + block.shape[1:])


def take(array, axis, index):
    return lax.index_in_dim(array, index, axis, keepdims=False)


def stage_sums(kept, got, axis):
    return tuple(add_low(take(kept, axis, i), take(got, axis, i)) for i in range(2))


def far_halves(part):
    pairs = part.reshape((part.shape[0] // 2, 2) + part.shape[1:])
    return pairs[:, 0], pairs[:, 1]


def scatter_far(part, stride, rows):
    while part.shape[0] > 1:
        keep, send = far_halves(part)
        got = flip(send, stride)
        if rows is not None:
            got, other = tied(got, flip(rows, stride))
            rows = rows + other
        part = add_low(keep, got) if part.shape[0] > 2 else keep.astype(F32) + got
        stride *= 2
    return part[0].astype(F32), rows


def tied(*values):
    return lax.optimization_barrier(values)


def shards(
    tokens,
    cotangent,
    lengths,
    dealing,
    w_query,
    w_key,
    w_value,
    w_out,
    b_query,
    b_value,
    b_out,
    norm1_gain,
    norm1_bias,
    w_up,
    b_up,
    w_down,
    b_down,
    norm2_gain,
    norm2_bias,
):
    devices = lax.axis_size("dev")
    me = lax.axis_index("dev")
    seq_count, local_len, width = tokens.shape
    per_device = seq_count // devices
    longest = local_len * devices
    capacity = cotangent.shape[0]
    share = w_query.shape[0]
    hidden = w_up.shape[1]

    outgoing = jnp.take(tokens, dealing, axis=0, mode="clip").reshape(devices, per_device, local_len, width)

    vectors = (
        b_query,
        b_value,
        b_out,
        norm1_gain,
        norm1_bias,
        b_down,
        norm2_gain,
        norm2_bias,
    )
    own_attn, own_ffn = prepare(
        me.reshape(1), (w_query, w_key, w_value, w_out), w_up, w_down, vectors, b_up
    )
    long = hidden // devices
    attn_line, ffn_line = gather_far(own_attn), gather_far(own_ffn)
    attn_line = jnp.stack(attn_line)
    attn_x, attn_y = plane_neighbours(attn_line)
    corner = attn_x[:, : 2 * share], attn_y[:, 2 * share :]
    outgoing, _, _, *ffn_line = tied(outgoing, *corner, *ffn_line)
    arrived = lax.all_to_all(outgoing, "dev", 0, 0)
    attn_own = (attn_line, attn_x, attn_y, *plane_corner(*corner))
    attn_pieces = (*attn_own, *(flip(block, 1) for block in attn_own))
    ffn_line = jnp.stack(ffn_line)
    ffn_x, ffn_y = plane_neighbours(ffn_line)

    my_slots = lax.dynamic_slice_in_dim(dealing, me * per_device, per_device)
    slot_len = jnp.take(lengths, my_slots)
    slot_ends = jnp.cumsum(slot_len)
    starts = slot_ends - slot_len
    row_ids = jnp.arange(capacity, dtype=jnp.int32)
    segment = jnp.sum((row_ids[:, None] >= slot_ends[None, :]).astype(jnp.int32), axis=1)
    is_valid = segment < per_device
    bounds = jnp.concatenate([starts, slot_ends[-1:]])
    picked = segment[:, None] == jnp.arange(per_device + 1, dtype=jnp.int32)[None, :]
    position = row_ids - jnp.sum(jnp.where(picked, bounds[None, :], 0), axis=1)
    source = (position // local_len) * (per_device * local_len) + segment * local_len
    source = jnp.where(is_valid, source + position % local_len, -1)

    packed, queries, key_rows, value_rows, vector_rows, weights = projections(
        me.reshape(1), devices, source, arrived.reshape(-1, width), attn_pieces
    )
    ffn_x, ffn_y, queries = tied(ffn_x, ffn_y, queries)
    corner = ffn_x[:, :long], ffn_y[:, long:]
    *corner, queries = tied(*corner, queries)
    ffn_corner = plane_corner(*corner)
    context, log_total, resid1 = attention_forward(
        segment, packed, vector_rows, queries, key_rows, value_rows, weights
    )
    *ffn_corner, resid1 = tied(*ffn_corner, resid1)
    ffn_own = (ffn_line, ffn_x, ffn_y, *ffn_corner)
    ffn_pieces = (*ffn_own, *(flip(block, 1) for block in ffn_own))

    layer_out, g_resid1, g_attn, g_rows, a_keep, a_send, b_keep, b_send = feed_forward(
        me.reshape(1), devices, hidden, slot_ends[-1:], resid1, cotangent, vector_rows, ffn_pieces
    )

    col_blocks = hidden // width
    own_far = devices // 8

    got_a, got_b = flip(a_send, 1), flip(b_send, 1)
    backward = partial(attention_backward, segment=segment, log_total=log_total, weights=weights)
    operands = dict(queries=queries, key_rows=key_rows, value_rows=value_rows)
    grads_0 = backward(0, 1, g_attn=g_attn, **operands)
    got_a, got_b, *grads_0 = tied(got_a, got_b, *grads_0)
    a_keep, a_send = stage_sums(near_shape(a_keep), near_shape(got_a), 2)
    b_keep, b_send = stage_sums(near_shape(b_keep), near_shape(got_b), 1)
    a_send, b_send, g_attn_late = tied(a_send, b_send, g_attn)
    got_a, got_b = flip(a_send, 2), flip(b_send, 4)
    grads_1 = backward(1, width // GROUP, g_attn=g_attn_late, **operands)
    step_ids = jnp.arange(longest, dtype=jnp.int32).reshape(devices, 1, local_len)
    inside = step_ids < slot_len[None, :, None]
    take_rows = jnp.where(inside, starts[None, :, None] + step_ids, -1).reshape(-1)
    gradients = (grads_0, grads_1)
    unpacked = input_gradient(take_rows, g_resid1, weights, gradients)
    got_a, got_b, unpacked, g_attn_late, *grads_1 = tied(
        got_a, got_b, unpacked, g_attn_late, *grads_1
    )
    returned = lax.all_to_all(
        unpacked.reshape(devices, per_device, local_len, width), "dev", 0, 0
    )
    a_keep, a_send = stage_sums(a_keep, got_a, 1)
    b_keep, b_send = stage_sums(b_keep, got_b, 1)
    got_a, got_b = flip(a_send, 4), flip(b_send, 2)

    c_keep, c_send, d_keep, d_send, g_rows_attn = weight_gradients(
        me.reshape(1), devices, packed, context, g_attn_late, (grads_0, grads_1)
    )
    g_rows = g_rows + jnp.pad(g_rows_attn, ((0, 8), (0, 0)))
    got_a, got_b, got_c, got_d, g_other = tied(
        got_a, got_b, flip(c_send, 1), flip(d_send, 1), flip(g_rows, 1)
    )
    ffn_part = jnp.concatenate(
        [
            add_low(a_keep, got_a),
            add_low(b_keep, got_b).reshape(own_far, -1, width),
        ],
        axis=1,
    )
    ffn_keep, ffn_send = far_halves(ffn_part)
    ffn_got = flip(ffn_send, 8)
    c_keep, c_send = stage_sums(near_shape(c_keep), near_shape(got_c), 2)
    d_keep, d_send = stage_sums(near_shape(d_keep), near_shape(got_d), 1)
    g_rows = g_rows + g_other
    got_c, got_d, g_other = tied(flip(c_send, 2), flip(d_send, 4), flip(g_rows, 2))
    c_keep, c_send = stage_sums(c_keep, got_c, 1)
    d_keep, d_send = stage_sums(d_keep, got_d, 1)
    g_rows = g_rows + g_other
    got_c, got_d, g_other, returned = tied(
        flip(c_send, 4), flip(d_send, 2), flip(g_rows, 4), returned
    )
    ffn_part = add_low(ffn_keep, ffn_got)
    attn_part = jnp.concatenate([add_low(c_keep, got_c), add_low(d_keep, got_d)], axis=1)
    g_rows = g_rows + g_other
    attn_keep, attn_send = far_halves(attn_part)
    attn_got, g_other = tied(flip(attn_send, 8), flip(g_rows, 8))
    attn_part = add_low(attn_keep, attn_got)
    g_rows = g_rows + g_other
    ffn_sum, _ = scatter_far(ffn_part, 16, None)
    attn_sum, g_rows = scatter_far(attn_part, 16, g_rows)
    g_wdown = ffn_sum[:long]
    g_wup = ffn_sum[long:].reshape(col_blocks, share, width)
    g_wup = g_wup.transpose(1, 0, 2).reshape(share, hidden)
    own_vec = lax.dynamic_slice_in_dim(g_rows[:8], me * share, share, axis=1)
    up_rows = g_rows[8 : 8 + col_blocks].reshape(hidden)
    own_up = lax.dynamic_slice_in_dim(up_rows, me * (hidden // devices), hidden // devices)

    slots = jnp.arange(seq_count, dtype=jnp.int32)
    inverse_deal = jnp.sum(jnp.where(dealing[None, :] == slots[:, None], slots[None, :], 0), axis=1)
    returned = returned.reshape(seq_count, local_len, width)
    input_grad = jnp.take(returned, inverse_deal, axis=0, mode="clip")
    return (
        layer_out,
        input_grad,
        attn_sum[0],
        attn_sum[1],
        attn_sum[2],
        attn_sum[3],
        own_vec[0],
        own_vec[1],
        own_vec[2],
        own_vec[3],
        own_vec[4],
        g_wup,
        own_up,
        g_wdown,
        own_vec[5],
        own_vec[6],
        own_vec[7],
    )


def solution(mesh):
    rows = P("dev", None)
    vector = P("dev")
    seqs = P(None, "dev", None)
    return jax.shard_map(
        shards,
        mesh=mesh,
        in_specs=(
            (seqs, rows, P(), P())
            + (rows,) * 4
            + (vector,) * 5
            + (rows, vector, rows)
            + (vector,) * 3
        ),
        out_specs=(
            (rows, seqs) + (rows,) * 4 + (vector,) * 5 + (rows, vector, rows) + (vector,) * 3
        ),
        check_vma=False,
    )
```

```python
from functools import partial

import jax
import jax.numpy as jnp
from jax import lax
from jax.experimental import pallas as pl
from jax.experimental.pallas import tpu as pltpu
from jax.sharding import PartitionSpec as P

HEADS = 12
HEAD_DIM = 64
PAIR = 2 * HEAD_DIM
GROUP = 4 * HEAD_DIM

MASKED_SCORE = -1e30
ROOT_HALF = 0.7071067811865476
INV_ROOT_TAU = 0.3989422804014327
BF16 = jnp.bfloat16
F32 = jnp.float32


def layer_norm(residual, norm_gain, norm_shift):
    center = residual - jnp.mean(residual, axis=-1, keepdims=True)
    inverse = lax.rsqrt(jnp.mean(center * center, axis=-1, keepdims=True) + 1e-05)
    normed = center * inverse
    return (normed * norm_gain + norm_shift, normed, inverse)


def norm_back(upstream, normed, inverse, norm_gain):
    scaled = upstream * norm_gain
    return inverse * (
        scaled
        - jnp.mean(scaled, axis=-1, keepdims=True)
        - normed * jnp.mean(scaled * normed, axis=-1, keepdims=True)
    )


def dot_nt(left, right):
    return lax.dot_general(left, right, (((1,), (1,)), ((), ())), preferred_element_type=F32)


def dot_nn(left, right):
    return lax.dot_general(left, right, (((1,), (0,)), ((), ())), preferred_element_type=F32)


def piece_blocks(devices, height, split):
    for core in range(2):
        for far in range(devices // 8):
            for near in range(4):
                relative = core + 2 * near + 8 * far
                if near < 3:
                    yield 5 * core + near, far, relative, 0, height
                else:
                    yield 5 * core + 3, far, relative, 0, split
                    yield 5 * core + 4, far, relative, split, height


def all_done(ref, sem):
    pltpu.make_async_copy(ref, ref, sem).wait()


def prepare_kernel(me_ref, *refs):
    weights, up_ref, down_ref, vectors, b_up = refs[:4], refs[4], refs[5], refs[6:14], refs[14]
    attn_ref, ffn_ref, rows_ref = refs[15:]
    share, width = weights[0].shape
    long = b_up.shape[1]
    me = me_ref[0]
    for i, weight in enumerate(weights):
        attn_ref[i * share : (i + 1) * share] = weight[...]
    ffn_ref[:long] = down_ref[...]
    for b in range(long // share):
        row = long + b * share
        ffn_ref[row : row + share] = up_ref[:, b * width : (b + 1) * width]
    rows_ref[...] = jnp.zeros_like(rows_ref)
    for i, vector in enumerate(vectors):
        rows_ref[i : i + 1, 0:share] = vector[...].astype(F32)
    for i in range(8, 16):
        rows_ref[i : i + 1, 0:long] = b_up[...].astype(F32)
    values = rows_ref[...].astype(BF16)
    shape = (values.shape[1], width)
    source = lax.broadcasted_iota(jnp.int32, shape, 0)
    target = lax.broadcasted_iota(jnp.int32, shape, 1)
    moved = []
    for start in (me * share, (me * long) % width):
        here = jnp.where(target == source + start, 1.0, 0.0).astype(BF16)
        moved.append(dot_nn(values, here))
    row = lax.broadcasted_iota(jnp.int32, moved[0].shape, 0)
    of_up = jnp.where(row == 8 + (me * long) // width, moved[1], 0.0)
    attn_ref[4 * share :] = jnp.where(row < 8, moved[0], of_up).astype(BF16)


def prepare(me, weights, w_up, w_down, vectors, b_up):
    share, width = weights[0].shape
    long = w_down.shape[0]
    vmem = pl.BlockSpec(memory_space=pltpu.VMEM)
    smem = pl.BlockSpec(memory_space=pltpu.SMEM)
    rows = [vector.reshape(1, -1) for vector in vectors + (b_up,)]
    return pl.pallas_call(
        prepare_kernel,
        in_specs=[smem] + [vmem] * 15,
        out_specs=[vmem] * 2,
        out_shape=[
            jax.ShapeDtypeStruct((4 * share + 16, width), BF16),
            jax.ShapeDtypeStruct((2 * long, width), BF16),
        ],
        scratch_shapes=[pltpu.VMEM((16, PAIR), F32)],
        cost_estimate=pl.CostEstimate(flops=1 << 22, transcendentals=0, bytes_accessed=1 << 20),
    )(me, *weights, w_up, w_down, *rows)


def projection_kernel(blocked, devices, me_ref, source_ref, arrived_ref, *refs):
    pieces, refs = (refs[:10], refs[10:]) if blocked else (refs[:2], refs[2:])
    packed_ref, q_ref, k_ref, v_ref, vec_ref, w_out_ref, weights, vec_rows, sems = refs
    rows, width = packed_ref.shape
    share = width // devices
    me = me_ref[0]
    if blocked:
        height = 4 * share + 16
        for array, far, relative, top, bottom in piece_blocks(devices, height, 2 * share):
            row = pl.multiple_of((relative ^ me) * share, 8)
            for i in range(top // share, min(bottom // share, 4)):
                pltpu.make_async_copy(
                    pieces[array].at[far, pl.ds(i * share - top, share)],
                    weights.at[i, pl.ds(row, share)],
                    sems.at[0],
                ).start()
            if bottom == height:
                pltpu.make_async_copy(
                    pieces[array].at[far, pl.ds(4 * share - top, 16)],
                    vec_rows.at[relative],
                    sems.at[1],
                ).start()
    else:
        pltpu.make_async_copy(pieces[0], weights, sems.at[0]).start()
        pltpu.make_async_copy(pieces[1], vec_rows, sems.at[1]).start()
    places = arrived_ref.shape[0]
    block = rows // 4
    for i in range(4):
        here = slice(i * block, (i + 1) * block)
        pick = source_ref[here] == lax.broadcasted_iota(jnp.int32, (block, places), 1)
        pick = jnp.where(pick, 1.0, 0.0).astype(BF16)
        packed_ref[here] = dot_nn(pick, arrived_ref[...]).astype(BF16)
    all_done(vec_rows, sems.at[1])
    vec_ref[...] = jnp.sum(vec_rows[...].astype(F32), axis=0)
    all_done(weights, sems.at[0])
    out_copy = pltpu.make_async_copy(weights, w_out_ref, sems.at[2])
    out_copy.start()
    packed = packed_ref[...]
    q_ref[...] = ((dot_nn(packed, weights[0]) + vec_ref[0:1, :]) * 0.125).astype(BF16)
    k_ref[...] = dot_nn(packed, weights[1]).astype(BF16)
    v_ref[...] = (dot_nn(packed, weights[2]) + vec_ref[1:2, :]).astype(BF16)
    out_copy.wait()


def attention_forward_kernel(
    seg_col, seg_row, packed_ref, vec_ref, q_ref, k_ref, v_ref, wo_ref, ctx_ref, lse_ref, resid_ref, bias
):
    step = pl.program_id(0)
    rows = q_ref.shape[0]

    @pl.when(step == 0)
    def _():
        bias[...] = jnp.where(seg_col[...] == seg_row[...], 0.0, MASKED_SCORE)
        resid_ref[...] = packed_ref[...].astype(F32) + vec_ref[2:3, :]

    lane = lax.broadcasted_iota(jnp.int32, (rows, PAIR), 1)
    stats = lse_ref[...]
    for pair in range(GROUP // PAIR):
        span = slice(pair * PAIR, (pair + 1) * PAIR)
        q_pair, k_pair, v_pair = q_ref[:, span], k_ref[:, span], v_ref[:, span]
        outs = []
        for half in range(2):
            own = (lane // HEAD_DIM) == half
            q_own = jnp.where(own, q_pair, jnp.zeros_like(q_pair))
            scores = dot_nt(q_own, k_pair) + bias[...]
            top = jnp.max(scores, axis=1, keepdims=True)
            exped = jnp.exp(scores - top)
            total = jnp.sum(exped, axis=1, keepdims=True)
            outs.append(dot_nn(exped.astype(BF16), v_pair) * (1.0 / total))
            head = step * (GROUP // HEAD_DIM) + pair * 2 + half
            stats = jnp.where(lane == head, top + jnp.log(total), stats)
        ctx_ref[:, span] = jnp.where(lane < HEAD_DIM, outs[0], outs[1]).astype(BF16)
    lse_ref[...] = stats
    resid_ref[...] += dot_nn(ctx_ref[...], wo_ref[...])


def natural(pieces):
    corners = [jnp.concatenate(pieces[i + 3 : i + 5], axis=1) for i in (0, 5)]
    blocks = jnp.stack(
        [b for i, corner in zip((0, 5), corners) for b in (*pieces[i : i + 3], corner)], axis=1
    )
    far = blocks.shape[0]
    blocks = blocks.reshape((far, 2, 4) + blocks.shape[2:]).swapaxes(1, 2)
    return in_order(blocks.reshape((8 * far,) + blocks.shape[3:]))


def projections(me, devices, source, arrived, pieces):
    rows, width = source.shape[0], arrived.shape[1]
    share = width // devices
    blocked = share % 8 == 0
    if not blocked:
        rows_of = natural(pieces)
        parts = [rows_of[:, i * share : (i + 1) * share].reshape(width, width) for i in range(4)]
        pieces = (jnp.stack(parts), rows_of[:, 4 * share :])
    vmem = pl.BlockSpec(memory_space=pltpu.VMEM)
    any_space = pl.BlockSpec(memory_space=pl.ANY)
    return pl.pallas_call(
        partial(projection_kernel, blocked, devices),
        in_specs=[pl.BlockSpec(memory_space=pltpu.SMEM), vmem, vmem] + [any_space] * len(pieces),
        out_specs=[vmem] * 5 + [any_space],
        out_shape=[jax.ShapeDtypeStruct((rows, width), BF16)] * 4
        + [
            jax.ShapeDtypeStruct((16, width), F32),
            jax.ShapeDtypeStruct((4, width, width), BF16),
        ],
        scratch_shapes=[
            pltpu.VMEM((4, width, width), BF16),
            pltpu.VMEM((devices, 16, width), BF16),
            pltpu.SemaphoreType.DMA((3,)),
        ],
        compiler_params=pltpu.CompilerParams(vmem_limit_bytes=40 << 20),
        cost_estimate=pl.CostEstimate(
            flops=6 * rows * width * width + 2 * rows * width * arrived.shape[0],
            transcendentals=0,
            bytes_accessed=16 * width * width + rows * width * 10,
        ),
    )(me, source[:, None], arrived, *pieces)


def attention_forward(segment, packed, vectors, queries, key_rows, value_rows, weights):
    rows, width = packed.shape
    block = pl.BlockSpec((rows, GROUP), lambda g: (0, g))
    whole = lambda shape: pl.BlockSpec(shape, lambda g: (0, 0))
    return pl.pallas_call(
        attention_forward_kernel,
        grid=(width // GROUP,),
        in_specs=[
            whole((rows, 1)),
            whole((1, rows)),
            whole((rows, width)),
            whole((16, width)),
            block,
            block,
            block,
            pl.BlockSpec((None, GROUP, width), lambda g: (3, g, 0)),
        ],
        out_specs=[block, whole((rows, PAIR)), whole((rows, width))],
        out_shape=[
            jax.ShapeDtypeStruct((rows, width), BF16),
            jax.ShapeDtypeStruct((rows, PAIR), F32),
            jax.ShapeDtypeStruct((rows, width), F32),
        ],
        scratch_shapes=[pltpu.VMEM((rows, rows), F32)],
        compiler_params=pltpu.CompilerParams(vmem_limit_bytes=48 << 20),
        cost_estimate=pl.CostEstimate(
            flops=HEADS * rows * rows * PAIR * 4 + 2 * rows * width * width,
            transcendentals=HEADS * rows * rows,
            bytes_accessed=2 * width * width + rows * width * 14,
        ),
    )(
        segment[:, None],
        segment[None, :],
        packed,
        vectors,
        queries,
        key_rows,
        value_rows,
        weights,
    )


def attention_backward_kernel(
    first,
    seg_col,
    seg_row,
    lse_ref,
    g_attn_ref,
    w_out_ref,
    q_ref,
    k_ref,
    v_ref,
    dq_ref,
    dk_ref,
    dv_ref,
    bias,
):
    step = pl.program_id(0)

    @pl.when(step == 0)
    def _():
        bias[...] = jnp.where(seg_col[...] == seg_row[...], 0.0, MASKED_SCORE)

    rows = q_ref.shape[0]
    lane = lax.broadcasted_iota(jnp.int32, (rows, PAIR), 1)
    g_context = dot_nt(g_attn_ref[...], w_out_ref[...]).astype(BF16)
    for pair in range(GROUP // PAIR):
        span = slice(pair * PAIR, (pair + 1) * PAIR)
        q_pair, k_pair, v_pair = q_ref[:, span], k_ref[:, span], v_ref[:, span]
        g_pair = g_context[:, span]
        q_turn, g_turn = q_pair.T, g_pair.T
        dq, dk, dv = [], [], []
        for half in range(2):
            own = (lane // HEAD_DIM) == half
            part = slice(half * HEAD_DIM, (half + 1) * HEAD_DIM)
            zero = jnp.zeros_like(q_pair)
            head = (first + step) * (GROUP // HEAD_DIM) + pair * 2 + half
            log_total = jnp.sum(jnp.where(lane == head, lse_ref[...], 0.0), axis=1, keepdims=True)
            scores = dot_nt(jnp.where(own, q_pair, zero), k_pair) + bias[...]
            probs = jnp.exp(scores - log_total)
            low = probs.astype(BF16)
            g_probs = dot_nt(jnp.where(own, g_pair, zero), v_pair)
            product = probs * g_probs
            g_scores = (product - probs * jnp.sum(product, axis=1, keepdims=True)).astype(BF16)
            dq.append(dot_nn(g_scores, k_pair))
            dk.append(dot_nn(q_turn[part], g_scores))
            dv.append(dot_nn(g_turn[part], low))
        dq_ref[:, span] = jnp.where(lane < HEAD_DIM, dq[0], dq[1]).astype(BF16)
        dk_ref[:, span] = jnp.concatenate(dk, axis=0).T.astype(BF16)
        dv_ref[:, span] = jnp.concatenate(dv, axis=0).T.astype(BF16)


def attention_backward(first, last, segment, log_total, g_attn, weights, queries, key_rows, value_rows):
    rows, width = queries.shape
    taken = pl.BlockSpec((rows, GROUP), lambda g: (0, g + first))
    made = pl.BlockSpec((rows, GROUP), lambda g: (0, g))
    whole = lambda shape: pl.BlockSpec(shape, lambda g: (0, 0))
    count = last - first
    return pl.pallas_call(
        partial(attention_backward_kernel, first),
        grid=(count,),
        in_specs=[
            whole((rows, 1)),
            whole((1, rows)),
            whole((rows, PAIR)),
            whole((rows, width)),
            pl.BlockSpec((None, GROUP, width), lambda g: (3, g + first, 0)),
        ]
        + [taken] * 3,
        out_specs=[made] * 3,
        out_shape=[jax.ShapeDtypeStruct((rows, count * GROUP), BF16)] * 3,
        scratch_shapes=[pltpu.VMEM((rows, rows), F32)],
        compiler_params=pltpu.CompilerParams(vmem_limit_bytes=48 << 20),
        cost_estimate=pl.CostEstimate(
            flops=count * 4 * rows * rows * PAIR * 10,
            transcendentals=count * 4 * rows * rows,
            bytes_accessed=count * rows * GROUP * 14,
        ),
    )(segment[:, None], segment[None, :], log_total, g_attn, weights, queries, key_rows, value_rows)


def input_gradient_kernel(parts, row_ref, resid_ref, w_ref, *refs):
    out_ref = refs[-1]
    rows = resid_ref.shape[0]
    total = resid_ref[...]
    column = 0
    for i in range(parts):
        dq, dk, dv = (refs[3 * i + j] for j in range(3))
        span = slice(column, column + dq.shape[1])
        column += dq.shape[1]
        total += dot_nt(dq[...], w_ref[0, :, span]) * 0.125
        total += dot_nt(dk[...], w_ref[1, :, span])
        total += dot_nt(dv[...], w_ref[2, :, span])
    g_input = total.astype(BF16)
    places = row_ref.shape[0]
    block = places // 4
    for i in range(4):
        here = slice(i * block, (i + 1) * block)
        pick = row_ref[here] == lax.broadcasted_iota(jnp.int32, (block, rows), 1)
        pick = jnp.where(pick, 1.0, 0.0).astype(BF16)
        out_ref[here] = dot_nn(pick, g_input).astype(BF16)


def input_gradient(take_rows, g_resid1, weights, gradients):
    rows, width = g_resid1.shape
    places = take_rows.shape[0]
    flat = [g for group in gradients for g in group]
    vmem = pl.BlockSpec(memory_space=pltpu.VMEM)
    return pl.pallas_call(
        partial(input_gradient_kernel, len(gradients)),
        in_specs=[vmem] * (3 + len(flat)),
        out_specs=vmem,
        out_shape=jax.ShapeDtypeStruct((places, width), BF16),
        compiler_params=pltpu.CompilerParams(vmem_limit_bytes=48 << 20),
        cost_estimate=pl.CostEstimate(
            flops=6 * rows * width * width + 2 * places * rows * width,
            transcendentals=0,
            bytes_accessed=12 * width * width + 10 * rows * width + 2 * places * width,
        ),
    )(take_rows[:, None], g_resid1, weights, *flat)


def paired_store(values, index, core, keep_ref, send_ref):
    low, high = values
    first = core == 0
    keep_ref[index] = jnp.where(first, low, high)
    send_ref[index] = jnp.where(first, high, low)


def weight_gradient_kernel(blocked, parts, me_ref, x_ref, ctx_ref, g_attn_ref, *refs):
    ins, outs = refs[: 3 * parts], refs[3 * parts :]
    rows, width = x_ref.shape
    me = me_ref[0]
    core = me & 1
    vec_ref = outs[-1]
    vec_ref[...] = jnp.zeros_like(vec_ref)

    def store(kind, grad):
        if not blocked:
            outs[0][kind] = grad
            return
        keep, send = (outs[2 * (kind // 2) + i] for i in range(2))
        share = keep.shape[2]
        for i in range(keep.shape[0]):
            low, high = (grad[(2 * i + j) * share : (2 * i + j + 1) * share] for j in range(2))
            paired_store((low, high), (i ^ (me >> 1), kind % 2), core, keep, send)

    x_turn = x_ref[...].T
    for j in range(3):
        pieces = []
        for i in range(parts):
            grads = ins[3 * i + j][...]
            span = slice(i * grads.shape[1], (i + 1) * grads.shape[1])
            piece = dot_nn(x_turn, grads)
            pieces.append((piece * 0.125 if j == 0 else piece).astype(BF16))
        store(j, jnp.concatenate(pieces, axis=1))
    store(3, dot_tn(ctx_ref[...], g_attn_ref[...]).astype(BF16))
    column = 0
    for i in range(parts):
        dq, _, dv = (ins[3 * i + j][...].astype(F32) for j in range(3))
        span = slice(column, column + dq.shape[1])
        column += dq.shape[1]
        vec_ref[0:1, span] = jnp.sum(dq, axis=0, keepdims=True) * 0.125
        vec_ref[1:2, span] = jnp.sum(dv, axis=0, keepdims=True)


def weight_gradients(me, devices, packed, context, g_attn, gradients):
    rows, width = packed.shape
    share = width // devices
    blocked = share % 8 == 0
    flat = [g for group in gradients for g in group]
    vmem = pl.BlockSpec(memory_space=pltpu.VMEM)
    smem = pl.BlockSpec(memory_space=pltpu.SMEM)
    if blocked:
        shapes = [jax.ShapeDtypeStruct((devices // 2, 2, share, width), BF16)] * 4
    else:
        shapes = [jax.ShapeDtypeStruct((4, width, width), BF16)]
    shapes.append(jax.ShapeDtypeStruct((8, width), F32))
    outs = pl.pallas_call(
        partial(weight_gradient_kernel, blocked, len(gradients)),
        in_specs=[smem] + [vmem] * (3 + len(flat)),
        out_specs=[vmem] * len(shapes),
        out_shape=shapes,
        compiler_params=pltpu.CompilerParams(vmem_limit_bytes=48 << 20),
        cost_estimate=pl.CostEstimate(
            flops=8 * rows * width * width,
            transcendentals=0,
            bytes_accessed=8 * width * width + 12 * rows * width,
        ),
    )(me, packed, context, g_attn, *flat)
    if blocked:
        return outs
    grads = in_order(outs[0].reshape(4, devices, share, width).transpose(1, 0, 2, 3))
    grads = grads.reshape(devices // 2, 2, 4, share, width)
    return [grads[:, i, j : j + 2] for j in (0, 2) for i in range(2)] + [outs[1]]


def dot_tn(left, right):
    return lax.dot_general(left, right, (((0,), (0,)), ((), ())), preferred_element_type=F32)


def feed_forward_kernel(blocked, devices, me_ref, count_ref, resid1_ref, cot_ref, vec_ref, *refs):
    pieces, refs = (refs[:10], refs[10:]) if blocked else (refs[:2], refs[2:])
    out_ref, g_resid1_ref, g_attn_ref, g_vec_ref = refs[:4]
    count = 4 if blocked else 2
    outs, refs = refs[4 : 4 + count], refs[4 + count :]
    made, refs = refs[:count], refs[count:]
    up, down, act, slope, low, acc, sems = refs
    rows, width = resid1_ref.shape
    blocks = up.shape[0]
    me = me_ref[0]
    share = width // devices
    long = share * blocks

    if blocked:
        for array, far, relative, top, bottom in piece_blocks(devices, 2 * long, long):
            piece = pieces[array].at[far]
            if bottom > long:
                row = pl.multiple_of((relative ^ me) * share, 8)
                for b in range(blocks):
                    pltpu.make_async_copy(
                        piece.at[pl.ds(long + b * share - top, share)],
                        up.at[b, pl.ds(row, share)],
                        sems.at[0],
                    ).start()
            if top == 0:
                row = pl.multiple_of((relative ^ me) * long, 8)
                pltpu.make_async_copy(
                    piece.at[pl.ds(0, long)], down.at[pl.ds(row, long)], sems.at[1]
                ).start()
    else:
        pltpu.make_async_copy(pieces[0], down, sems.at[1]).start()
        pltpu.make_async_copy(pieces[1], up, sems.at[0]).start()

    gain_one, shift_one, bdown, gain_two, shift_two = (vec_ref[i : i + 1, :] for i in range(3, 8))
    hidden1, normed1, inverse1 = layer_norm(resid1_ref[...], gain_one, shift_one)
    low[...] = hidden1.astype(BF16)
    acc[...] = hidden1 + bdown
    all_done(up, sems.at[0])

    def forward(b, carry):
        pre = dot_nn(low[...], up[b]) + vec_ref[pl.ds(8 + b, 1), :]
        cdf = 0.5 * (1.0 + lax.erf(pre * ROOT_HALF))
        slope[b] = cdf + pre * (jnp.exp(-0.5 * pre * pre) * INV_ROOT_TAU)
        activated = (pre * cdf).astype(BF16)
        if b == 0:
            all_done(down, sems.at[1])
        act[b] = activated
        acc[...] += dot_nn(activated, down[pl.ds(pl.multiple_of(b * width, width), width)])
        return carry

    for b in range(blocks):
        forward(b, 0)

    g_vec_ref[...] = jnp.zeros_like(g_vec_ref)
    result, normed2, inverse2 = layer_norm(acc[...], gain_two, shift_two)
    valid = lax.broadcasted_iota(jnp.int32, (rows, 1), 0) < count_ref[0]
    out_ref[...] = jnp.where(valid, result, 0.0).astype(BF16)
    g_out = jnp.where(valid, cot_ref[...].astype(F32), 0.0)
    g_vec_ref[6:7, :] = jnp.sum(g_out * normed2, axis=0, keepdims=True)
    g_vec_ref[7:8, :] = jnp.sum(g_out, axis=0, keepdims=True)
    g_resid2 = norm_back(g_out, normed2, inverse2, gain_two)
    acc[...] = g_resid2
    g_ffn = g_resid2.astype(BF16)
    g_vec_ref[5:6, :] = jnp.sum(g_ffn.astype(F32), axis=0, keepdims=True)

    def backward(b, carry):
        start = pl.multiple_of(b * width, width)
        down_b = down[pl.ds(start, width)]
        g_down = dot_tn(act[b], g_ffn).astype(BF16)
        if blocked:
            per = width // long // 2
            for i in range(per):
                pair = (g_down[(2 * i + j) * long : (2 * i + j + 1) * long] for j in range(2))
                index = (b * per + i) ^ (me >> 1)
                paired_store(pair, index, me & 1, *made[:2])
                for k in range(2):
                    pltpu.make_async_copy(
                        made[k].at[index], outs[k].at[index], sems.at[2 + k]
                    ).start()
        else:
            made[0][pl.ds(start, width)] = g_down
        g_pre = (dot_nt(g_ffn, down_b) * slope[b]).astype(BF16)
        g_vec_ref[pl.ds(8 + b, 1), :] = jnp.sum(g_pre.astype(F32), axis=0, keepdims=True)
        g_up = dot_tn(low[...], g_pre).astype(BF16)
        if blocked:
            for i in range(devices // 2):
                pair = (g_up[(2 * i + j) * share : (2 * i + j + 1) * share] for j in range(2))
                index = i ^ (me >> 1)
                paired_store(pair, (index, b), me & 1, *made[2:])
                for k in range(2, 4):
                    pltpu.make_async_copy(
                        made[k].at[index, b], outs[k].at[index, b], sems.at[2 + k]
                    ).start()
        else:
            made[1][b] = g_up
        acc[...] += dot_nt(g_pre, up[b])
        return carry

    for b in range(blocks):
        backward(b, 0)
    if not blocked:
        for k in range(2):
            pltpu.make_async_copy(made[k], outs[k], sems.at[2 + k]).start()
    g_hidden1 = acc[...]
    g_vec_ref[3:4, :] = jnp.sum(g_hidden1 * normed1, axis=0, keepdims=True)
    g_vec_ref[4:5, :] = jnp.sum(g_hidden1, axis=0, keepdims=True)
    g_resid1 = norm_back(g_hidden1, normed1, inverse1, gain_one)
    g_resid1_ref[...] = g_resid1
    g_attn = g_resid1.astype(BF16)
    g_attn_ref[...] = g_attn
    g_vec_ref[2:3, :] = jnp.sum(g_attn.astype(F32), axis=0, keepdims=True)
    for k in range(count):
        all_done(made[k], sems.at[2 + k])


def feed_forward(me, devices, hidden, count, resid1, cotangent, vectors, pieces):
    rows, width = resid1.shape
    share = width // devices
    blocks = hidden // width
    long = hidden // devices
    blocked = share % 8 == 0
    if blocked:
        g_shapes = [(devices // 2, long, width)] * 2 + [(devices // 2, blocks, share, width)] * 2
    else:
        rows_of = natural(pieces)
        up = rows_of[:, long:].reshape(devices, blocks, share, width).transpose(1, 0, 2, 3)
        pieces = (rows_of[:, :long].reshape(hidden, width), up.reshape(blocks, width, width))
        g_shapes = [(hidden, width), (blocks, width, width)]
    vmem = pl.BlockSpec(memory_space=pltpu.VMEM)
    smem = pl.BlockSpec(memory_space=pltpu.SMEM)
    any_space = pl.BlockSpec(memory_space=pl.ANY)
    outs = pl.pallas_call(
        partial(feed_forward_kernel, blocked, devices),
        in_specs=[smem, smem] + [vmem] * 3 + [any_space] * len(pieces),
        out_specs=[vmem] * 4 + [any_space] * len(g_shapes),
        out_shape=[
            jax.ShapeDtypeStruct((rows, width), BF16),
            jax.ShapeDtypeStruct((rows, width), F32),
            jax.ShapeDtypeStruct((rows, width), BF16),
            jax.ShapeDtypeStruct((16, width), F32),
        ]
        + [jax.ShapeDtypeStruct(shape, BF16) for shape in g_shapes],
        scratch_shapes=[pltpu.VMEM(shape, BF16) for shape in g_shapes]
        + [
            pltpu.VMEM((blocks, width, width), BF16),
            pltpu.VMEM((hidden, width), BF16),
            pltpu.VMEM((blocks, rows, width), BF16),
            pltpu.VMEM((blocks, rows, width), F32),
            pltpu.VMEM((rows, width), BF16),
            pltpu.VMEM((rows, width), F32),
            pltpu.SemaphoreType.DMA((6,)),
        ],
        compiler_params=pltpu.CompilerParams(vmem_limit_bytes=60 << 20),
        cost_estimate=pl.CostEstimate(
            flops=12 * rows * width * hidden,
            transcendentals=2 * rows * hidden,
            bytes_accessed=8 * width * hidden + 16 * rows * width,
        ),
    )(me, count, resid1, cotangent, vectors, *pieces)
    if blocked:
        return outs
    g_down = in_order(outs[4].reshape(devices, long, width))
    g_up = in_order(outs[5].reshape(blocks, devices, share, width).transpose(1, 0, 2, 3))
    pairs = [g.reshape((devices // 2, 2) + g.shape[1:]) for g in (g_down, g_up)]
    return list(outs[:4]) + [g[:, i] for g in pairs for i in range(2)]


def flip(array, stride):
    devices = lax.axis_size("dev")
    return lax.ppermute(array, "dev", [(i, i ^ stride) for i in range(devices)])


def gather_far(shard):
    blocks = [shard]
    for k in range(1, lax.axis_size("dev") // 8):
        low = k & -k
        blocks.append(flip(blocks[k - low], 8 * low))
    return blocks


def plane_neighbours(line):
    return flip(line, 2), flip(line, 4)


def plane_corner(across_x, across_y):
    return flip(across_x, 4), flip(across_y, 2)


def in_order(blocks):
    devices = blocks.shape[0]
    order = jnp.arange(devices, dtype=jnp.int32) ^ lax.axis_index("dev")
    return jnp.take(blocks, order, axis=0, mode="clip")


def add_low(left, right):
    return (left.astype(F32) + right.astype(F32)).astype(BF16)


def near_shape(block):
    return block.reshape((block.shape[0] // 4, 2, 2) + block.shape[1:])


def take(array, axis, index):
    return lax.index_in_dim(array, index, axis, keepdims=False)


def low_sum(*parts):
    return sum(part.astype(F32) for part in parts).astype(BF16)


def sent(terms, axis):
    return low_sum(*(take(term, axis, 1) for term in terms))


def held(terms, axis):
    return [take(term, axis, 0) for term in terms]


def far_halves(part):
    pairs = part.reshape((part.shape[0] // 2, 2) + part.shape[1:])
    return pairs[:, 0], pairs[:, 1]


def scatter_far(part, stride, rows):
    while part.shape[0] > 1:
        keep, send = far_halves(part)
        got = flip(send, stride)
        if rows is not None:
            got, other = tied(got, flip(rows, stride))
            rows = rows + other
        part = add_low(keep, got) if part.shape[0] > 2 else keep.astype(F32) + got
        stride *= 2
    return part[0].astype(F32), rows


def tied(*values):
    return lax.optimization_barrier(values)


def shards(
    tokens,
    cotangent,
    lengths,
    dealing,
    w_query,
    w_key,
    w_value,
    w_out,
    b_query,
    b_value,
    b_out,
    norm1_gain,
    norm1_bias,
    w_up,
    b_up,
    w_down,
    b_down,
    norm2_gain,
    norm2_bias,
):
    devices = lax.axis_size("dev")
    me = lax.axis_index("dev")
    seq_count, local_len, width = tokens.shape
    per_device = seq_count // devices
    longest = local_len * devices
    capacity = cotangent.shape[0]
    share = w_query.shape[0]
    hidden = w_up.shape[1]

    outgoing = jnp.take(tokens, dealing, axis=0, mode="clip").reshape(devices, per_device, local_len, width)

    vectors = (
        b_query,
        b_value,
        b_out,
        norm1_gain,
        norm1_bias,
        b_down,
        norm2_gain,
        norm2_bias,
    )
    own_attn, own_ffn = prepare(
        me.reshape(1), (w_query, w_key, w_value, w_out), w_up, w_down, vectors, b_up
    )
    long = hidden // devices
    attn_line, ffn_line = gather_far(own_attn), gather_far(own_ffn)
    attn_line = jnp.stack(attn_line)
    attn_x, attn_y = plane_neighbours(attn_line)
    corner = attn_x[:, : 2 * share], attn_y[:, 2 * share :]
    outgoing, _, _, *ffn_line = tied(outgoing, *corner, *ffn_line)
    arrived = lax.all_to_all(outgoing, "dev", 0, 0)
    attn_own = (attn_line, attn_x, attn_y, *plane_corner(*corner))
    attn_pieces = (*attn_own, *(flip(block, 1) for block in attn_own))
    ffn_line = jnp.stack(ffn_line)
    ffn_x, ffn_y = plane_neighbours(ffn_line)

    my_slots = lax.dynamic_slice_in_dim(dealing, me * per_device, per_device)
    slot_len = jnp.take(lengths, my_slots)
    slot_ends = jnp.cumsum(slot_len)
    starts = slot_ends - slot_len
    row_ids = jnp.arange(capacity, dtype=jnp.int32)
    segment = jnp.sum((row_ids[:, None] >= slot_ends[None, :]).astype(jnp.int32), axis=1)
    is_valid = segment < per_device
    bounds = jnp.concatenate([starts, slot_ends[-1:]])
    picked = segment[:, None] == jnp.arange(per_device + 1, dtype=jnp.int32)[None, :]
    position = row_ids - jnp.sum(jnp.where(picked, bounds[None, :], 0), axis=1)
    source = (position // local_len) * (per_device * local_len) + segment * local_len
    source = jnp.where(is_valid, source + position % local_len, -1)

    packed, queries, key_rows, value_rows, vector_rows, weights = projections(
        me.reshape(1), devices, source, arrived.reshape(-1, width), attn_pieces
    )
    ffn_x, ffn_y, queries = tied(ffn_x, ffn_y, queries)
    corner = ffn_x[:, :long], ffn_y[:, long:]
    *corner, queries = tied(*corner, queries)
    ffn_corner = plane_corner(*corner)
    context, log_total, resid1 = attention_forward(
        segment, packed, vector_rows, queries, key_rows, value_rows, weights
    )
    *ffn_corner, resid1 = tied(*ffn_corner, resid1)
    ffn_own = (ffn_line, ffn_x, ffn_y, *ffn_corner)
    ffn_pieces = (*ffn_own, *(flip(block, 1) for block in ffn_own))

    layer_out, g_resid1, g_attn, g_rows, a_keep, a_send, b_keep, b_send = feed_forward(
        me.reshape(1), devices, hidden, slot_ends[-1:], resid1, cotangent, vector_rows, ffn_pieces
    )

    col_blocks = hidden // width
    own_far = devices // 8

    got_a, got_b = flip(a_send, 1), flip(b_send, 1)
    backward = partial(attention_backward, segment=segment, log_total=log_total, weights=weights)
    operands = dict(queries=queries, key_rows=key_rows, value_rows=value_rows)
    grads_0 = backward(0, 1, g_attn=g_attn, **operands)
    got_a, got_b, *grads_0 = tied(got_a, got_b, *grads_0)
    a_terms = [near_shape(a_keep), near_shape(got_a)]
    b_terms = [near_shape(b_keep), near_shape(got_b)]
    a_send, b_send = sent(a_terms, 2), sent(b_terms, 1)
    a_terms, b_terms = held(a_terms, 2), held(b_terms, 1)
    a_send, b_send, g_attn_late = tied(a_send, b_send, g_attn)
    got_a, got_b = flip(a_send, 2), flip(b_send, 4)
    grads_1 = backward(1, width // GROUP, g_attn=g_attn_late, **operands)
    step_ids = jnp.arange(longest, dtype=jnp.int32).reshape(devices, 1, local_len)
    inside = step_ids < slot_len[None, :, None]
    take_rows = jnp.where(inside, starts[None, :, None] + step_ids, -1).reshape(-1)
    gradients = (grads_0, grads_1)
    unpacked = input_gradient(take_rows, g_resid1, weights, gradients)
    got_a, got_b, unpacked, g_attn_late, *grads_1 = tied(
        got_a, got_b, unpacked, g_attn_late, *grads_1
    )
    returned = lax.all_to_all(
        unpacked.reshape(devices, per_device, local_len, width), "dev", 0, 0
    )
    a_terms, b_terms = a_terms + [got_a], b_terms + [got_b]
    a_send, b_send = sent(a_terms, 1), sent(b_terms, 1)
    a_terms, b_terms = held(a_terms, 1), held(b_terms, 1)
    got_a, got_b = flip(a_send, 4), flip(b_send, 2)

    c_keep, c_send, d_keep, d_send, g_rows_attn = weight_gradients(
        me.reshape(1), devices, packed, context, g_attn_late, (grads_0, grads_1)
    )
    g_rows = g_rows + jnp.pad(g_rows_attn, ((0, 8), (0, 0)))
    got_a, got_b, got_c, got_d, g_other = tied(
        got_a, got_b, flip(c_send, 1), flip(d_send, 1), flip(g_rows, 1)
    )
    ffn_part = jnp.concatenate(
        [
            low_sum(*a_terms, got_a),
            low_sum(*b_terms, got_b).reshape(own_far, -1, width),
        ],
        axis=1,
    )
    ffn_keep, ffn_send = far_halves(ffn_part)
    ffn_got = flip(ffn_send, 8)
    c_terms = [near_shape(c_keep), near_shape(got_c)]
    d_terms = [near_shape(d_keep), near_shape(got_d)]
    c_send, d_send = sent(c_terms, 2), sent(d_terms, 1)
    c_terms, d_terms = held(c_terms, 2), held(d_terms, 1)
    g_rows = g_rows + g_other
    got_c, got_d, g_other = tied(flip(c_send, 2), flip(d_send, 4), flip(g_rows, 2))
    c_terms, d_terms = c_terms + [got_c], d_terms + [got_d]
    c_send, d_send = sent(c_terms, 1), sent(d_terms, 1)
    c_terms, d_terms = held(c_terms, 1), held(d_terms, 1)
    g_rows = g_rows + g_other
    got_c, got_d, g_other, returned = tied(
        flip(c_send, 4), flip(d_send, 2), flip(g_rows, 4), returned
    )
    ffn_part = add_low(ffn_keep, ffn_got)
    attn_part = jnp.concatenate([low_sum(*c_terms, got_c), low_sum(*d_terms, got_d)], axis=1)
    g_rows = g_rows + g_other
    attn_keep, attn_send = far_halves(attn_part)
    attn_got, g_other = tied(flip(attn_send, 8), flip(g_rows, 8))
    attn_part = add_low(attn_keep, attn_got)
    g_rows = g_rows + g_other
    ffn_sum, _ = scatter_far(ffn_part, 16, None)
    attn_sum, g_rows = scatter_far(attn_part, 16, g_rows)
    g_wdown = ffn_sum[:long]
    g_wup = ffn_sum[long:].reshape(col_blocks, share, width)
    g_wup = g_wup.transpose(1, 0, 2).reshape(share, hidden)
    own_vec = lax.dynamic_slice_in_dim(g_rows[:8], me * share, share, axis=1)
    up_rows = g_rows[8 : 8 + col_blocks].reshape(hidden)
    own_up = lax.dynamic_slice_in_dim(up_rows, me * (hidden // devices), hidden // devices)

    slots = jnp.arange(seq_count, dtype=jnp.int32)
    inverse_deal = jnp.sum(jnp.where(dealing[None, :] == slots[:, None], slots[None, :], 0), axis=1)
    returned = returned.reshape(seq_count, local_len, width)
    input_grad = jnp.take(returned, inverse_deal, axis=0, mode="clip")
    return (
        layer_out,
        input_grad,
        attn_sum[0],
        attn_sum[1],
        attn_sum[2],
        attn_sum[3],
        own_vec[0],
        own_vec[1],
        own_vec[2],
        own_vec[3],
        own_vec[4],
        g_wup,
        own_up,
        g_wdown,
        own_vec[5],
        own_vec[6],
        own_vec[7],
    )


def solution(mesh):
    rows = P("dev", None)
    vector = P("dev")
    seqs = P(None, "dev", None)
    return jax.shard_map(
        shards,
        mesh=mesh,
        in_specs=(
            (seqs, rows, P(), P())
            + (rows,) * 4
            + (vector,) * 5
            + (rows, vector, rows)
            + (vector,) * 3
        ),
        out_specs=(
            (rows, seqs) + (rows,) * 4 + (vector,) * 5 + (rows, vector, rows) + (vector,) * 3
        ),
        check_vma=False,
    )
```
